32 devices in a mesh: parts: 2 (over y), seq: 4 (over z), head: 4 (over x, core).
Axes of the slice: x: 2, y: 2, z: 4, core: 2. Of those that a mesh axis runs over, the one named last changes fastest.
Arguments:
- hidden: bfloat16 [48, 12288], P(('parts', 'head'), 'seq'), parts along dimension 0, may hold values from -600 to 600
- norm_gain: float32 [12288], P('seq'), may hold values from 0.1 to 1.9
- w_query: bfloat16 [12288, 12288], P('seq', 'head'), may hold values from -0.0546875 to 0.0546875
- w_key: bfloat16 [12288, 1024], P('seq', 'head'), may hold values from -0.0546875 to 0.0546875
- w_value: bfloat16 [12288, 1024], P('seq', 'head'), may hold values from -0.0546875 to 0.0546875
- w_out: bfloat16 [12288, 12288], P('head', 'seq'), may hold values from -0.0546875 to 0.0546875
- lengths: int32 [48], P('parts'), parts along dimension 0, may hold values from 1 to 512, as said below
- key_cache: bfloat16 [48, 8, 512, 128], P('parts', 'head', 'seq'), parts along dimension 0, may hold values from -600 to 600, as said below
- value_cache: bfloat16 [48, 8, 512, 128], P('parts', 'head', 'seq'), parts along dimension 0, may hold values from -6 to 6
Outputs:
- attn_out: bfloat16 [48, 12288], P(('parts', 'head'), 'seq'), parts along dimension 0
The draws below stay inside these ranges and needn't reach their ends.
There are 2 independent parts, one for each index of `parts`. The reference program is written for one: setup_inputs(seed, part) draws one part's arguments, and reference() takes and returns one part's arrays. A program takes and returns all parts, laid end to end along the dimension named above; an argument that names none is the same for every part. Nothing has to cross between parts.
Inputs may be any that keep to these rules, and one draw needn't show every extreme that they name: Sequence b holds lengths[b] cached tokens at positions 0 to lengths[b] - 1; its new token takes position lengths[b]. `key_cache`: positions at or past a sequence's length hold no data.
All inputs are finite; a program needn't handle non-finite values.
Results may differ from the reference program's by a relative error of at most 0.0075.
The reference program's roundings to bfloat16 on the way (of `scaled`, `queries`, `weights` and `mixed`) count: a program that leaves them out, or rounds other values in their place, can miss the bound.
Values may be sent and summed in bfloat16 or wider, within the bound.
A program may use at most 128 MiB of HBM per device.

```python
import jax
import jax.numpy as jnp
from jax import lax

D = 12288
HEADS = 96
KV_HEADS = 8
HD = 128
BATCH = 24
CTX_DEV = 128
GROUP = 12
CACHE = 512
N_SEQ = 4


def draw_hidden(key, part):
    first, second = jax.random.split(jax.random.fold_in(key, 11), 2)
    column = jnp.exp(jnp.log(10.0) * jnp.arange(D, dtype=jnp.float32) / (D - 1))
    rough = jax.random.uniform(second, (BATCH, D), jnp.float32, 0.7, 1.4)
    drawn = jnp.clip(jax.random.normal(first, (BATCH, D), jnp.float32), -5.0, 5.0)
    return jnp.clip(drawn * column * rough, -600.0, 600.0).astype(jnp.bfloat16)


def draw_lengths(key, part):
    first, second, third = jax.random.split(jax.random.fold_in(key, 23), 3)
    top_bits = CACHE.bit_length() - 1
    shifts = jnp.maximum(jax.random.randint(first, (BATCH,), -top_bits, top_bits + 1), 0)
    upper = jnp.right_shift(jnp.full((BATCH,), CACHE, jnp.int32), shifts.astype(jnp.int32))
    upper = jnp.maximum(upper, 1)
    drawn = jax.random.randint(second, (BATCH,), upper // 2 + 1, upper + 1)
    chosen = jax.random.randint(third, (), 0, BATCH)
    return jnp.where(jnp.arange(BATCH) == chosen, CACHE, drawn).astype(jnp.int32)


def draw_key_cache(key, part):
    first = jax.random.fold_in(jax.random.fold_in(key, 37), 0)
    drawn = 2.5 * jax.random.normal(first, (BATCH, KV_HEADS, CACHE, HD), jnp.float32)
    return jnp.clip(drawn, -15.0, 15.0).astype(jnp.bfloat16)


def level_of(rng, dims, shards, low, largest):
    def one(dim, shards_of):
        steps = jax.random.uniform(jax.random.fold_in(jax.random.fold_in(rng, 6), dim), (shards_of,), jnp.float32, low / len(shards), largest / len(shards))
        return jnp.repeat(jnp.exp(steps), dims[dim] // shards_of).reshape((-1,) + (1,) * (len(dims) - dim - 1))

    loudness = one(*shards[0])
    for cut in shards[1:]:
        loudness = loudness * one(*cut)
    return loudness


def normal_values(stream_key, dims, scale, reach, shards=(), held_as=jnp.bfloat16):
    values = scale * jax.random.normal(stream_key, dims, jnp.float32)
    if shards:
        values = values * level_of(stream_key, dims, shards, -0.22, 0.18)
    return jnp.clip(values, -reach, reach).astype(held_as)


def setup_inputs(seed: int = 0, part: int = 0) -> dict:
    keys = jax.random.split(jax.random.key(seed), 10)
    part_splits = jax.random.split(jax.random.fold_in(keys[9], part), 10)
    return {
        "hidden": draw_hidden(jax.random.fold_in(jax.random.fold_in(keys[9], part), 71), part),
        "norm_gain": jnp.clip(1.0 + 0.18 * jax.random.normal(keys[1], (D,), jnp.float32), 0.1, 1.9),
        "w_query": normal_values(keys[2], (D, HEADS * HD), D ** -0.5, 0.0546875, ((0, 4), (1, 4))),
        "w_key": normal_values(keys[3], (D, KV_HEADS * HD), D ** -0.5, 0.0546875, ((0, 4), (1, 4))),
        "w_value": normal_values(keys[4], (D, KV_HEADS * HD), D ** -0.5, 0.0546875, ((0, 4), (1, 4))),
        "w_out": normal_values(keys[5], (HEADS * HD, D), (HEADS * HD) ** -0.5, 0.0546875, ((0, 4), (1, 4))),
        "lengths": draw_lengths(jax.random.fold_in(jax.random.fold_in(keys[9], part), 71), part),
        "key_cache": draw_key_cache(jax.random.fold_in(jax.random.fold_in(keys[9], part), 71), part),
        "value_cache": normal_values(part_splits[8], (BATCH, KV_HEADS, CACHE, HD), 1.0, 6.0, ((1, 4), (2, 4))),
    }


EPSILON = 1e-05

def reference(hidden, norm_gain, w_query, w_key, w_value, w_out, lengths, key_cache, value_cache):
    widened = hidden.astype(jnp.float32)
    mean_square = lax.optimization_barrier(jnp.mean(widened * widened, axis=1, keepdims=True))
    inverse_rms = lax.rsqrt(mean_square + EPSILON)
    scaled = (widened * norm_gain).astype(jnp.bfloat16)
    query_full = jnp.dot(scaled, w_query, preferred_element_type=jnp.float32)
    queries = (query_full * inverse_rms * HD ** (-0.5)).astype(jnp.bfloat16)
    new_keys = (jnp.dot(scaled, w_key, preferred_element_type=jnp.float32) * inverse_rms).astype(jnp.bfloat16)
    new_values = (jnp.dot(scaled, w_value, preferred_element_type=jnp.float32) * inverse_rms).astype(jnp.bfloat16)
    grouped = queries.reshape(BATCH, KV_HEADS, GROUP, HD).transpose(1, 0, 2, 3)
    positions = jnp.arange(CACHE, dtype=jnp.int32)
    live_mask = positions[None, None, :] < lengths.astype(jnp.int32)[:, None, None]
    live_block = live_mask.reshape(BATCH, 1, N_SEQ, CTX_DEV)

    def per_head(operands):
        head_keys, head_values, head_query, new_key, new_value = operands
        scores = jnp.einsum('bgd,bpd->bgp', head_query.astype(jnp.float32), head_keys.astype(jnp.float32), precision=lax.Precision.HIGHEST)
        masked = jnp.where(live_mask, scores, -1e+30)
        blocked = masked.reshape(BATCH, GROUP, N_SEQ, CTX_DEV)
        block_max = lax.optimization_barrier(jnp.max(blocked, axis=-1))
        shifted = scores.reshape(BATCH, GROUP, N_SEQ, CTX_DEV) - block_max[..., None]
        weights = jnp.where(live_block, jnp.exp(jnp.where(live_block, shifted, 0.0)), 0.0).astype(jnp.bfloat16)
        block_den = lax.optimization_barrier(jnp.sum(weights.astype(jnp.float32), axis=-1))
        block_acc = jnp.einsum('bgcp,bcpd->bgcd', weights.astype(jnp.float32), head_values.reshape(BATCH, N_SEQ, CTX_DEV, HD).astype(jnp.float32), precision=lax.Precision.HIGHEST)
        self_score = lax.optimization_barrier(jnp.sum(head_query.astype(jnp.float32) * new_key.astype(jnp.float32)[:, None, :], axis=-1))
        top_score = jnp.maximum(lax.optimization_barrier(jnp.max(block_max, axis=-1)), self_score)
        factors = jnp.exp(block_max - top_score[..., None])
        own_weight = jnp.exp(self_score - top_score)
        denominator = lax.optimization_barrier(jnp.sum(factors * block_den, axis=-1)) + own_weight
        numerator = lax.optimization_barrier(jnp.sum(factors[..., None] * block_acc, axis=2)) + own_weight[..., None] * new_value.astype(jnp.float32)[:, None, :]
        return (numerator / denominator[..., None]).astype(jnp.bfloat16)
    attended = lax.map(per_head, (key_cache.transpose(1, 0, 2, 3), value_cache.transpose(1, 0, 2, 3), grouped, new_keys.reshape(BATCH, KV_HEADS, HD).transpose(1, 0, 2), new_values.reshape(BATCH, KV_HEADS, HD).transpose(1, 0, 2)))
    mixed = attended.transpose(1, 0, 2, 3).reshape(BATCH, HEADS * HD)
    return jnp.dot(mixed, w_out, preferred_element_type=jnp.float32).astype(jnp.bfloat16)
```

```python
import functools

import jax
import jax.numpy as jnp
from jax import lax
from jax.experimental import pallas as pl
from jax.experimental.pallas import tpu as pltpu
from jax.sharding import PartitionSpec as P

D = 12288


EPSILON = 1e-05


def joined(value, axis, join):
    pieces = jax.tree.map(lambda part: lax.all_gather(part, axis), value)
    head = jax.tree.map(lambda part: part[0], pieces)
    tail = jax.tree.map(lambda part: part[1:], pieces)
    subtotal, _ = lax.scan(lambda subtotal, slab: (join(subtotal, slab), None), head, tail)
    return subtotal


def join_parts(earlier, later):
    new_max = jnp.maximum(earlier[0], later[0])
    left_factor = jnp.exp(earlier[0] - new_max)
    right_factor = jnp.exp(later[0] - new_max)
    den_total = earlier[1] * left_factor + later[1] * right_factor
    acc_total = earlier[2] * left_factor[..., None] + later[2] * right_factor[..., None]
    return (new_max, den_total, acc_total)


def local(hidden, norm_gain, w_query, w_key, w_value, w_out, lengths, key_cache, value_cache):
    batch_size, kv_local, block_len, head_size = key_cache.shape
    group_size = w_query.shape[1] // (kv_local * head_size)
    token_rows = lax.all_gather(hidden, "head", axis=0, tiled=True)
    widened = token_rows.astype(jnp.float32)
    square_local = jnp.sum(widened * widened, axis=1)
    scaled = (widened * norm_gain).astype(jnp.bfloat16)
    query_part = jnp.dot(scaled, w_query, preferred_element_type=jnp.float32)
    key_part = jnp.dot(scaled, w_key, preferred_element_type=jnp.float32)
    value_part = jnp.dot(scaled, w_value, preferred_element_type=jnp.float32)
    query_factor = float(head_size) ** (-0.5)
    norm_total = lax.psum(square_local, "seq")
    query_sum, key_sum, value_sum = lax.psum((query_part, key_part, value_part), "seq")
    inverse_rms = lax.rsqrt(norm_total / D + EPSILON)[:, None]
    queries = (query_sum * inverse_rms * query_factor).astype(jnp.bfloat16)
    new_keys = (key_sum * inverse_rms).astype(jnp.bfloat16)
    new_values = (value_sum * inverse_rms).astype(jnp.bfloat16)
    grouped = queries.reshape(batch_size, kv_local, group_size, head_size)
    scores = jnp.einsum("bkgd,bkpd->bkgp", grouped, key_cache, preferred_element_type=jnp.float32)
    offset = lax.axis_index("seq") * block_len
    positions = offset + jnp.arange(block_len, dtype=jnp.int32)
    live_mask = (positions[None, :] < lengths[:, None])[:, None, None, :]
    block_max = jnp.max(jnp.where(live_mask, scores, -1e30), axis=-1)
    shifted = jnp.where(live_mask, scores - block_max[..., None], 0.0)
    weights = jnp.where(live_mask, jnp.exp(shifted), 0.0).astype(jnp.bfloat16)
    block_den = jnp.sum(weights.astype(jnp.float32), axis=-1)
    block_acc = jnp.einsum(
        "bkgp,bkpd->bkgd", weights, value_cache, preferred_element_type=jnp.float32
    )
    self_score = jnp.einsum(
        "oips,ois->oip",
        grouped,
        new_keys.reshape(batch_size, kv_local, head_size),
        preferred_element_type=jnp.float32,
    )
    global_max, den_merged, acc_merged = joined(
        (block_max, block_den, block_acc), "seq", join_parts
    )
    top_score = jnp.maximum(global_max, self_score)
    factors = jnp.exp(global_max - top_score)
    den_sum = den_merged * factors
    acc_sum = acc_merged * factors[..., None]
    own_weight = jnp.exp(self_score - top_score)
    denominator = den_sum + own_weight
    numerator = acc_sum + own_weight[..., None] * new_values.reshape(
        batch_size, kv_local, 1, head_size
    ).astype(jnp.float32)
    mixed = (
        (numerator / denominator[..., None])
        .astype(jnp.bfloat16)
        .reshape(batch_size, kv_local * group_size * head_size)
    )
    output = lax.psum_scatter(
        jnp.dot(mixed, w_out, preferred_element_type=jnp.float32),
        "head",
        scatter_dimension=0,
        tiled=True,
    )
    return output.astype(jnp.bfloat16)


MESH = pl.DeviceIdType.MESH


def layer_kernel(
    n_seq, n_head, hid, gain, lens, wq, wk, wv, wo, kc, vc, out,
    hid_buf, x_scr, xs_scr, len_scr, wq_buf, wkv_buf, wo_buf, kc_buf, vc_buf,
    part, rs_buf, ag_buf, q_scr, sc_scr, acc_scr, st_buf, ra_buf, mix_buf, o_acc, o_send, o_recv,
    load_sem, hid_send, hid_recv, rs_send, rs_recv, ag_send, ag_recv,
    st_send, st_recv, ra_send, ra_recv, mx_send, mx_recv, os_sem, or_sem,
):
    f32, bf16 = jnp.float32, jnp.bfloat16
    seq, hd = lax.axis_index("seq"), lax.axis_index("head")
    rows, feat = hid.shape
    batch, kv, block, size = kc.shape
    heads = wq.shape[1] // size
    group = heads // kv
    own = heads // n_seq
    width = own * size
    tile = 256 if width % 256 == 0 else size
    kv_cols = kv * size

    def load(index, source, target):
        copy = pltpu.make_async_copy(source, target, load_sem.at[index])
        copy.start()
        return copy

    def to(axis, index, source, target, send, recv):
        return pltpu.make_async_remote_copy(
            src_ref=source, dst_ref=target, send_sem=send, recv_sem=recv,
            device_id={axis: index}, device_id_type=MESH,
        )

    seq_to = [lax.rem(seq + j + 1, n_seq) for j in range(n_seq)]
    seq_from = [lax.rem(seq + n_seq - j - 1, n_seq) for j in range(n_seq)]
    head_to = [lax.rem(hd + j + 1, n_head) for j in range(n_head)]

    own_hidden = load(0, hid, hid_buf.at[hd])
    key_load = load(1, wk, wkv_buf.at[:, pl.ds(0, kv_cols)])
    value_load = load(2, wv, wkv_buf.at[:, pl.ds(kv_cols, kv_cols)])
    q_loads = [
        load(3 + j, wq.at[:, pl.ds(pl.multiple_of(seq_to[j] * width, width), width)], wq_buf.at[j])
        for j in range(n_seq)
    ]
    base = 3 + n_seq
    kc_load = load(base, kc, kc_buf)
    vc_load = load(base + 1, vc, vc_buf)
    o_loads = [
        load(base + 2 + j, wo.at[pl.ds(j * width, width)], wo_buf.at[j]) for j in range(n_seq)
    ]

    barrier = pltpu.get_barrier_semaphore()
    for j in range(n_head - 1):
        pl.semaphore_signal(barrier, inc=1, device_id={"head": head_to[j]}, device_id_type=MESH)
    for j in range(n_seq - 1):
        pl.semaphore_signal(barrier, inc=1, device_id={"seq": seq_to[j]}, device_id_type=MESH)
    pl.semaphore_wait(barrier, n_head + n_seq - 2)

    hid_copies = [
        to("head", head_to[j], hid, hid_buf.at[hd], hid_send.at[j], hid_recv.at[j])
        for j in range(n_head - 1)
    ]
    for copy in hid_copies:
        copy.start()
    for b in range(batch):
        len_scr[b : b + 1, :] = jnp.full((1, block), lens[b], jnp.int32)
    own_hidden.wait()
    for copy in hid_copies:
        copy.wait_recv()
    for j in range(n_head):
        x_scr[j * rows : (j + 1) * rows, :] = hid_buf[j].astype(f32)
    widened = x_scr[...]
    square = jnp.sum(widened * widened, axis=1, keepdims=True)
    xs_scr[...] = (widened * gain[...]).astype(bf16)

    key_load.wait()
    value_load.wait()
    rs_copies = []
    for j in range(n_seq):
        q_loads[j].wait()

        @pl.loop(0, width // tile)
        def _(n):
            cols = pl.ds(pl.multiple_of(n * tile, tile), tile)
            part[j, :, cols] = jnp.dot(xs_scr[...], wq_buf[j, :, cols], preferred_element_type=f32)

        kv_at = pl.ds(pl.multiple_of(seq_to[j] * size, size), size)
        part[j, :, width : width + size] = jnp.dot(
            xs_scr[...], wkv_buf[:, kv_at], preferred_element_type=f32
        )
        part[j, :, width + size :] = jnp.broadcast_to(square, (batch, 128))
        if j < n_seq - 1:
            copy = to("seq", seq_to[j], part.at[j], rs_buf.at[j], rs_send.at[j], rs_recv.at[j])
            copy.start()
            rs_copies.append(copy)

    for copy in rs_copies:
        copy.wait_recv()

    def summed(cols):
        total = part[n_seq - 1, :, cols]
        for j in range(n_seq - 1):
            total = total + rs_buf[j, :, cols]
        return total

    mean_square = summed(slice(width + size, width + size + 128)) / (feat * n_seq)
    inverse_rms = lax.rsqrt(mean_square + EPSILON)[:, :1]
    factor = float(size) ** (-0.5)
    ag_buf[seq, :, :width] = (summed(slice(0, width)) * inverse_rms * factor).astype(bf16)
    ag_buf[seq, :, width:] = (summed(slice(width, width + size)) * inverse_rms).astype(bf16)
    ag_copies = []
    for j in range(n_seq - 1):
        copy = to("seq", seq_to[j], ag_buf.at[seq], ag_buf.at[seq], ag_send.at[j], ag_recv.at[j])
        copy.start()
        ag_copies.append(copy)
    kc_load.wait()
    vc_load.wait()
    for copy in ag_copies:
        copy.wait_recv()
    for s in range(n_seq):
        for i in range(own):
            at = (s * own + i) * batch
            q_scr[at : at + batch, :] = ag_buf[s, :, i * size : (i + 1) * size].astype(f32)

    unroll = 4 if batch % 4 == 0 else 1

    @pl.loop(0, batch // unroll)
    def _(step):
        for u in range(unroll):
            b = step * unroll + u
            for k in range(kv):
                at = pl.ds(k * group * batch + b, group, stride=batch)
                sc_scr[at, :] = lax.dot_general(
                    q_scr[at, :].astype(bf16), kc_buf[b, k], (((1,), (1,)), ((), ())),
                    preferred_element_type=f32,
                )

    lane = lax.broadcasted_iota(jnp.int32, (batch, block), 1)
    live = lane + seq * block < len_scr[...]
    stats = jnp.zeros((batch, 128), f32)
    for h in range(heads):
        scores = sc_scr[h * batch : (h + 1) * batch, :]
        top = jnp.max(jnp.where(live, scores, -1e30), axis=1, keepdims=True)
        shifted = jnp.where(live, scores - top, 0.0)
        weights = jnp.where(live, jnp.exp(shifted), 0.0).astype(bf16).astype(f32)
        sc_scr[h * batch : (h + 1) * batch, :] = weights
        total = jnp.sum(weights, axis=1, keepdims=True)
        stats = jnp.where(lane == h, top, jnp.where(lane == 64 + h, total, stats))
    st_buf[n_seq - 1] = stats
    st_copies = []
    for j in range(n_seq - 1):
        copy = to("seq", seq_to[j], st_buf.at[n_seq - 1], st_buf.at[j], st_send.at[j], st_recv.at[j])
        copy.start()
        st_copies.append(copy)

    @pl.loop(0, batch // unroll)
    def _(step):
        for u in range(unroll):
            b = step * unroll + u
            for k in range(kv):
                at = pl.ds(k * group * batch + b, group, stride=batch)
                acc_scr[at, :] = jnp.dot(
                    sc_scr[at, :].astype(bf16), vc_buf[b, k], preferred_element_type=f32
                )

    ra_copies = []
    part_rows = own * batch
    for j in range(n_seq - 1):
        at = pl.ds(pl.multiple_of(seq_to[j] * part_rows, part_rows), part_rows)
        copy = to("seq", seq_to[j], acc_scr.at[at], ra_buf.at[j], ra_send.at[j], ra_recv.at[j])
        copy.start()
        ra_copies.append(copy)

    kv_head = (seq * own) // group
    new_key = ag_buf[kv_head, :, width:].astype(f32)
    new_value = ag_buf[kv + kv_head, :, width:].astype(f32)
    own_at = pl.multiple_of(seq * part_rows, part_rows)
    self_score = jnp.zeros((batch, 128), f32)
    for i in range(own):
        query = q_scr[pl.ds(own_at + i * batch, batch), :]
        score = jnp.sum(query * new_key, axis=1, keepdims=True)
        self_score = jnp.where(lane == i, score, self_score)
    for copy in st_copies:
        copy.wait_recv()
    shift = lax.rem(128 - seq * own, 128)
    maxes = [pltpu.roll(st_buf[j], shift, 1) for j in range(n_seq)]
    dens = [pltpu.roll(m, 64, 1) for m in maxes]
    top_score = self_score
    for m in maxes:
        top_score = jnp.maximum(top_score, m)
    factors = [jnp.exp(m - top_score) for m in maxes]
    own_weight = jnp.exp(self_score - top_score)
    denominator = own_weight
    for f, d in zip(factors, dens):
        denominator = denominator + f * d
    own_weight = own_weight / denominator
    factors = [f / denominator for f in factors]
    for copy in ra_copies:
        copy.wait_recv()
    for i in range(own):
        mixed = own_weight[:, i : i + 1] * new_value
        mixed += factors[n_seq - 1][:, i : i + 1] * acc_scr[pl.ds(own_at + i * batch, batch), :]
        for j in range(n_seq - 1):
            mixed += factors[j][:, i : i + 1] * ra_buf[j, i * batch : (i + 1) * batch, :]
        mix_buf[seq, :, i * size : (i + 1) * size] = mixed.astype(bf16)
    mx_copies = []
    for j in range(n_seq - 1):
        copy = to("seq", seq_to[j], mix_buf.at[seq], mix_buf.at[seq], mx_send.at[j], mx_recv.at[j])
        copy.start()
        mx_copies.append(copy)
    for copy in o_loads:
        copy.wait()

    columns = wo.shape[1]
    o_tile = 256 if columns % (4 * 256) == 0 else 128
    chunks = 4 if columns % (4 * o_tile) == 0 else 1
    chunk = columns // chunks
    order = [seq] + seq_from[: n_seq - 1]
    o_copies = []
    for j in range(n_seq):
        if j > 0:
            mx_copies[j - 1].wait_recv()
        source = order[j]
        if j < n_seq - 1:

            @pl.loop(0, columns // o_tile)
            def _(n):
                cols = pl.ds(pl.multiple_of(n * o_tile, o_tile), o_tile)
                value = jnp.dot(mix_buf[source], wo_buf[source, :, cols], preferred_element_type=f32)
                o_acc[:, cols] = value if j == 0 else o_acc[:, cols] + value

            continue
        for c in range(chunks):

            @pl.loop(0, chunk // o_tile)
            def _(n):
                cols = pl.ds(pl.multiple_of(c * chunk + n * o_tile, o_tile), o_tile)
                value = jnp.dot(mix_buf[source], wo_buf[source, :, cols], preferred_element_type=f32)
                o_acc[:, cols] = o_acc[:, cols] + value
                for r in range(n_head):
                    o_send[r, :, cols] = o_acc[r * rows : (r + 1) * rows, cols]

            cols = pl.ds(c * chunk, chunk)
            for r in range(n_head - 1):
                copy = to(
                    "head", head_to[r], o_send.at[head_to[r], :, cols], o_recv.at[r, :, cols],
                    os_sem.at[c * n_head + r], or_sem.at[c * n_head + r],
                )
                copy.start()
                o_copies.append(copy)
    for c in range(chunks):
        cols = slice(c * chunk, (c + 1) * chunk)
        for r in range(n_head - 1):
            o_copies[c * (n_head - 1) + r].wait_recv()
        total = o_send[hd, :, cols]
        for r in range(n_head - 1):
            total = total + o_recv[r, :, cols]
        out[:, cols] = total.astype(bf16)
    for copy in hid_copies + rs_copies + ag_copies + st_copies + ra_copies + mx_copies + o_copies:
        copy.wait_send()


def fused(n_seq, n_head, hidden, norm_gain, w_query, w_key, w_value, w_out, lengths, key_cache, value_cache):
    rows, feat = hidden.shape
    batch, kv, block, size = key_cache.shape
    heads = w_query.shape[1] // size
    own = heads // n_seq
    width = own * size
    columns = w_out.shape[1]
    f32, bf16 = jnp.float32, jnp.bfloat16
    hbm = pl.BlockSpec(memory_space=pl.ANY)
    vmem = pl.BlockSpec(memory_space=pltpu.VMEM)
    smem = pl.BlockSpec(memory_space=pltpu.SMEM)
    dma = pltpu.SemaphoreType.DMA
    steps = [dma((n_seq,)), dma((n_seq,))]
    return pl.pallas_call(
        functools.partial(layer_kernel, n_seq, n_head),
        out_shape=jax.ShapeDtypeStruct((rows, columns), bf16),
        in_specs=[hbm, vmem, smem] + [hbm] * 6,
        out_specs=vmem,
        scratch_shapes=[
            pltpu.VMEM((n_head, rows, feat), bf16),
            pltpu.VMEM((batch, feat), f32),
            pltpu.VMEM((batch, feat), bf16),
            pltpu.VMEM((batch, block), jnp.int32),
            pltpu.VMEM((n_seq, feat, width), bf16),
            pltpu.VMEM((feat, 2 * kv * size), bf16),
            pltpu.VMEM((n_seq, width, columns), bf16),
            pltpu.VMEM(key_cache.shape, bf16),
            pltpu.VMEM(value_cache.shape, bf16),
            pltpu.VMEM((n_seq, batch, width + size + 128), f32),
            pltpu.VMEM((n_seq - 1, batch, width + size + 128), f32),
            pltpu.VMEM((n_seq, batch, width + size), bf16),
            pltpu.VMEM((heads * batch, size), f32),
            pltpu.VMEM((heads * batch, block), f32),
            pltpu.VMEM((heads * batch, size), f32),
            pltpu.VMEM((n_seq, batch, 128), f32),
            pltpu.VMEM((n_seq - 1, own * batch, size), f32),
            pltpu.VMEM((n_seq, batch, width), bf16),
            pltpu.VMEM((batch, columns), f32),
            pltpu.VMEM((n_head, rows, columns), f32),
            pltpu.VMEM((n_head - 1, rows, columns), f32),
            dma((5 + 2 * n_seq,)),
            dma((n_head,)),
            dma((n_head,)),
            *steps, *steps, *steps, *steps, *steps,
            dma((4 * n_head,)),
            dma((4 * n_head,)),
        ],
        compiler_params=pltpu.CompilerParams(
            collective_id=0, has_side_effects=True, vmem_limit_bytes=60 * 1024 * 1024
        ),
    )(hidden, norm_gain.reshape(1, feat), lengths, w_query, w_key, w_value, w_out, key_cache, value_cache)


def program(n_seq, n_head, *args):
    w_query, key_cache = args[2], args[7]
    batch, kv, block, size = key_cache.shape
    heads = w_query.shape[1] // size
    own = max(heads // n_seq, 1)
    fits = (
        own * n_seq == heads
        and (heads // kv) % own == 0
        and 2 * kv == n_seq
        and size == 128
        and block == 128
        and heads <= 64
        and batch % 8 == 0
    )
    return fused(n_seq, n_head, *args) if fits else local(*args)


def solution(mesh):
    return jax.shard_map(
        functools.partial(program, mesh.shape["seq"], mesh.shape["head"]),
        mesh=mesh,
        in_specs=(
            P(("parts", "head"), "seq"),
            P("seq"),
            P("seq", "head"),
            P("seq", "head"),
            P("seq", "head"),
            P("head", "seq"),
            P("parts"),
            P("parts", "head", "seq", None),
            P("parts", "head", "seq", None),
        ),
        out_specs=P(("parts", "head"), "seq"),
        check_vma=False,
    )
```

```python
import functools

import jax
import jax.numpy as jnp
from jax import lax
from jax.experimental import pallas as pl
from jax.experimental.pallas import tpu as pltpu
from jax.sharding import PartitionSpec as P

D = 12288


EPSILON = 1e-05


def joined(value, axis, join):
    pieces = jax.tree.map(lambda part: lax.all_gather(part, axis), value)
    head = jax.tree.map(lambda part: part[0], pieces)
    tail = jax.tree.map(lambda part: part[1:], pieces)
    subtotal, _ = lax.scan(lambda subtotal, slab: (join(subtotal, slab), None), head, tail)
    return subtotal


def join_parts(earlier, later):
    new_max = jnp.maximum(earlier[0], later[0])
    left_factor = jnp.exp(earlier[0] - new_max)
    right_factor = jnp.exp(later[0] - new_max)
    den_total = earlier[1] * left_factor + later[1] * right_factor
    acc_total = earlier[2] * left_factor[..., None] + later[2] * right_factor[..., None]
    return (new_max, den_total, acc_total)


def local(hidden, norm_gain, w_query, w_key, w_value, w_out, lengths, key_cache, value_cache):
    batch_size, kv_local, block_len, head_size = key_cache.shape
    group_size = w_query.shape[1] // (kv_local * head_size)
    token_rows = lax.all_gather(hidden, "head", axis=0, tiled=True)
    widened = token_rows.astype(jnp.float32)
    square_local = jnp.sum(widened * widened, axis=1)
    scaled = (widened * norm_gain).astype(jnp.bfloat16)
    query_part = jnp.dot(scaled, w_query, preferred_element_type=jnp.float32)
    key_part = jnp.dot(scaled, w_key, preferred_element_type=jnp.float32)
    value_part = jnp.dot(scaled, w_value, preferred_element_type=jnp.float32)
    query_factor = float(head_size) ** (-0.5)
    norm_total = lax.psum(square_local, "seq")
    query_sum, key_sum, value_sum = lax.psum((query_part, key_part, value_part), "seq")
    inverse_rms = lax.rsqrt(norm_total / D + EPSILON)[:, None]
    queries = (query_sum * inverse_rms * query_factor).astype(jnp.bfloat16)
    new_keys = (key_sum * inverse_rms).astype(jnp.bfloat16)
    new_values = (value_sum * inverse_rms).astype(jnp.bfloat16)
    grouped = queries.reshape(batch_size, kv_local, group_size, head_size)
    scores = jnp.einsum("bkgd,bkpd->bkgp", grouped, key_cache, preferred_element_type=jnp.float32)
    offset = lax.axis_index("seq") * block_len
    positions = offset + jnp.arange(block_len, dtype=jnp.int32)
    live_mask = (positions[None, :] < lengths[:, None])[:, None, None, :]
    block_max = jnp.max(jnp.where(live_mask, scores, -1e30), axis=-1)
    shifted = jnp.where(live_mask, scores - block_max[..., None], 0.0)
    weights = jnp.where(live_mask, jnp.exp(shifted), 0.0).astype(jnp.bfloat16)
    block_den = jnp.sum(weights.astype(jnp.float32), axis=-1)
    block_acc = jnp.einsum(
        "bkgp,bkpd->bkgd", weights, value_cache, preferred_element_type=jnp.float32
    )
    self_score = jnp.einsum(
        "oips,ois->oip",
        grouped,
        new_keys.reshape(batch_size, kv_local, head_size),
        preferred_element_type=jnp.float32,
    )
    global_max, den_merged, acc_merged = joined(
        (block_max, block_den, block_acc), "seq", join_parts
    )
    top_score = jnp.maximum(global_max, self_score)
    factors = jnp.exp(global_max - top_score)
    den_sum = den_merged * factors
    acc_sum = acc_merged * factors[..., None]
    own_weight = jnp.exp(self_score - top_score)
    denominator = den_sum + own_weight
    numerator = acc_sum + own_weight[..., None] * new_values.reshape(
        batch_size, kv_local, 1, head_size
    ).astype(jnp.float32)
    mixed = (
        (numerator / denominator[..., None])
        .astype(jnp.bfloat16)
        .reshape(batch_size, kv_local * group_size * head_size)
    )
    output = lax.psum_scatter(
        jnp.dot(mixed, w_out, preferred_element_type=jnp.float32),
        "head",
        scatter_dimension=0,
        tiled=True,
    )
    return output.astype(jnp.bfloat16)


MESH = pl.DeviceIdType.MESH


def layer_kernel(
    n_seq, n_head, hid, gain, lens, wq, wk, wv, wo, kc, vc, out,
    hid_buf, x_scr, xs_scr, len_scr, wq_buf, wkv_buf, wo_buf, kc_buf, vc_buf,
    part, rs_buf, sq_buf, ag_buf, nk_buf, q_scr, sc_scr, acc_scr, st_buf, acc_send, ra_buf, mix_buf, o_acc, o_own, o_send, o_recv,
    load_sem, hid_send, hid_recv, rs_send, rs_recv, sq_send, sq_recv, ag_send, ag_recv, nk_send, nk_recv,
    st_send, st_recv, ra_send, ra_recv, mx_send, mx_recv, os_sem, or_sem,
):
    f32, bf16 = jnp.float32, jnp.bfloat16
    seq, hd = lax.axis_index("seq"), lax.axis_index("head")
    rows, feat = hid.shape
    batch, kv, block, size = kc.shape
    heads = wq.shape[1] // size
    group = heads // kv
    own = heads // n_seq
    width = own * size
    kv_cols = kv * size

    def load(index, source, target):
        copy = pltpu.make_async_copy(source, target, load_sem.at[index])
        copy.start()
        return copy

    def to(axis, index, source, target, send, recv):
        return pltpu.make_async_remote_copy(
            src_ref=source, dst_ref=target, send_sem=send, recv_sem=recv,
            device_id={axis: index}, device_id_type=MESH,
        )

    seq_to = [lax.rem(seq + j + 1, n_seq) for j in range(n_seq)]
    seq_from = [lax.rem(seq + n_seq - j - 1, n_seq) for j in range(n_seq)]
    head_to = [lax.rem(hd + j + 1, n_head) for j in range(n_head)]

    own_hidden = load(0, hid, hid_buf.at[hd])
    barrier = pltpu.get_barrier_semaphore()
    for j in range(n_head - 1):
        pl.semaphore_signal(barrier, inc=1, device_id={"head": head_to[j]}, device_id_type=MESH)
    for j in range(n_seq - 1):
        pl.semaphore_signal(barrier, inc=1, device_id={"seq": seq_to[j]}, device_id_type=MESH)
    key_load = load(1, wk, wkv_buf.at[:, pl.ds(0, kv_cols)])
    value_load = load(2, wv, wkv_buf.at[:, pl.ds(kv_cols, kv_cols)])
    q_loads = [
        load(3 + j, wq.at[:, pl.ds(pl.multiple_of(seq_to[j] * width, width), width)], wq_buf.at[j])
        for j in range(n_seq)
    ]
    base = 3 + n_seq
    kc_load = load(base, kc, kc_buf)
    vc_load = load(base + 1, vc, vc_buf)
    o_loads = [
        load(base + 2 + j, wo.at[pl.ds(j * width, width)], wo_buf.at[j]) for j in range(n_seq)
    ]

    own_hidden.wait()
    pl.semaphore_wait(barrier, n_head + n_seq - 2)

    hid_copies = [
        to("head", head_to[j], hid_buf.at[hd], hid_buf.at[hd], hid_send.at[j], hid_recv.at[j])
        for j in range(n_head - 1)
    ]
    for copy in hid_copies:
        copy.start()
    for b in range(batch):
        len_scr[b : b + 1, :] = jnp.full((1, block), lens[b], jnp.int32)
    for copy in hid_copies:
        copy.wait_recv()
    for j in range(n_head):
        x_scr[j * rows : (j + 1) * rows, :] = hid_buf[j].astype(f32)
    widened = x_scr[...]
    square = jnp.sum(widened * widened, axis=1, keepdims=True)
    sq_buf[n_seq - 1] = jnp.broadcast_to(square, (batch, 128))
    sq_copies = []
    for j in range(n_seq - 1):
        copy = to("seq", seq_to[j], sq_buf.at[n_seq - 1], sq_buf.at[j], sq_send.at[j], sq_recv.at[j])
        copy.start()
        sq_copies.append(copy)
    xs_scr[...] = (widened * gain[...]).astype(bf16)

    key_load.wait()
    value_load.wait()
    rs_copies = []
    for j in range(n_seq):
        q_loads[j].wait()

        part[j, :, :width] = jnp.dot(xs_scr[...], wq_buf[j], preferred_element_type=f32)
        kv_at = pl.ds(pl.multiple_of(seq_to[j] * size, size), size)
        part[j, :, width:] = jnp.dot(
            xs_scr[...], wkv_buf[:, kv_at], preferred_element_type=f32
        )
        if j < n_seq - 1:
            copy = to("seq", seq_to[j], part.at[j], rs_buf.at[j], rs_send.at[j], rs_recv.at[j])
            copy.start()
            rs_copies.append(copy)

    for copy in rs_copies:
        copy.wait_recv()

    def summed(cols):
        total = part[n_seq - 1, :, cols]
        for j in range(n_seq - 1):
            total = total + rs_buf[j, :, cols]
        return total

    for copy in sq_copies:
        copy.wait_recv()
    square_sum = sq_buf[0]
    for j in range(1, n_seq):
        square_sum = square_sum + sq_buf[j]
    mean_square = square_sum / (feat * n_seq)
    inverse_rms = lax.rsqrt(mean_square + EPSILON)[:, :1]
    factor = float(size) ** (-0.5)
    ag_buf[seq] = (summed(slice(0, width)) * inverse_rms * factor).astype(bf16)
    ag_copies = []
    for j in range(n_seq - 1):
        copy = to("seq", seq_to[j], ag_buf.at[seq], ag_buf.at[seq], ag_send.at[j], ag_recv.at[j])
        copy.start()
        ag_copies.append(copy)
    nk_buf[seq] = (summed(slice(width, width + size)) * inverse_rms).astype(bf16)
    nk_copies = []
    for j in range(n_seq - 1):
        copy = to("seq", seq_to[j], nk_buf.at[seq], nk_buf.at[seq], nk_send.at[j], nk_recv.at[j])
        copy.start()
        nk_copies.append(copy)
    kc_load.wait()
    vc_load.wait()
    for copy in ag_copies:
        copy.wait_recv()
    for s in range(n_seq):
        for i in range(own):
            at = (s * own + i) * batch
            q_scr[at : at + batch, :] = ag_buf[s, :, i * size : (i + 1) * size].astype(f32)

    unroll = 4 if batch % 4 == 0 else 1

    @pl.loop(0, batch // unroll)
    def _(step):
        for u in range(unroll):
            b = step * unroll + u
            for k in range(kv):
                at = pl.ds(k * group * batch + b, group, stride=batch)
                sc_scr[at, :] = lax.dot_general(
                    q_scr[at, :].astype(bf16), kc_buf[b, k], (((1,), (1,)), ((), ())),
                    preferred_element_type=f32,
                )

    lane = lax.broadcasted_iota(jnp.int32, (batch, block), 1)
    live = lane + seq * block < len_scr[...]
    stats = jnp.zeros((batch, 128), f32)
    for h in range(heads):
        scores = sc_scr[h * batch : (h + 1) * batch, :]
        top = jnp.max(jnp.where(live, scores, -1e30), axis=1, keepdims=True)
        shifted = jnp.where(live, scores - top, 0.0)
        weights = jnp.where(live, jnp.exp(shifted), 0.0).astype(bf16).astype(f32)
        sc_scr[h * batch : (h + 1) * batch, :] = weights
        total = jnp.sum(weights, axis=1, keepdims=True)
        stats = jnp.where(lane == h, top, jnp.where(lane == 64 + h, total, stats))
    st_buf[n_seq - 1] = stats
    st_copies = []
    for j in range(n_seq - 1):
        copy = to("seq", seq_to[j], st_buf.at[n_seq - 1], st_buf.at[j], st_send.at[j], st_recv.at[j])
        copy.start()
        st_copies.append(copy)

    @pl.loop(0, batch // unroll)
    def _(step):
        for u in range(unroll):
            b = step * unroll + u
            for k in range(kv):
                at = pl.ds(k * group * batch + b, group, stride=batch)
                acc_scr[at, :] = jnp.dot(
                    sc_scr[at, :].astype(bf16), vc_buf[b, k], preferred_element_type=f32
                )

    ra_copies = []
    part_rows = own * batch
    for j in range(n_seq - 1):
        at = pl.ds(pl.multiple_of(seq_to[j] * part_rows, part_rows), part_rows)
        acc_send[j] = acc_scr[at, :].astype(bf16)
        copy = to("seq", seq_to[j], acc_send.at[j], ra_buf.at[j], ra_send.at[j], ra_recv.at[j])
        copy.start()
        ra_copies.append(copy)

    kv_head = (seq * own) // group
    for copy in nk_copies:
        copy.wait_recv()
    new_key = nk_buf[kv_head].astype(f32)
    new_value = nk_buf[kv + kv_head].astype(f32)
    own_at = pl.multiple_of(seq * part_rows, part_rows)
    self_score = jnp.zeros((batch, 128), f32)
    for i in range(own):
        query = q_scr[pl.ds(own_at + i * batch, batch), :]
        score = jnp.sum(query * new_key, axis=1, keepdims=True)
        self_score = jnp.where(lane == i, score, self_score)
    for copy in st_copies:
        copy.wait_recv()
    shift = lax.rem(128 - seq * own, 128)
    maxes = [pltpu.roll(st_buf[j], shift, 1) for j in range(n_seq)]
    dens = [pltpu.roll(m, 64, 1) for m in maxes]
    top_score = self_score
    for m in maxes:
        top_score = jnp.maximum(top_score, m)
    factors = [jnp.exp(m - top_score) for m in maxes]
    own_weight = jnp.exp(self_score - top_score)
    denominator = own_weight
    for f, d in zip(factors, dens):
        denominator = denominator + f * d
    own_weight = own_weight / denominator
    factors = [f / denominator for f in factors]
    for copy in ra_copies:
        copy.wait_recv()
    for i in range(own):
        mixed = own_weight[:, i : i + 1] * new_value
        mixed += factors[n_seq - 1][:, i : i + 1] * acc_scr[pl.ds(own_at + i * batch, batch), :]
        for j in range(n_seq - 1):
            mixed += factors[j][:, i : i + 1] * ra_buf[j, i * batch : (i + 1) * batch, :].astype(f32)
        mix_buf[seq, :, i * size : (i + 1) * size] = mixed.astype(bf16)
    mx_copies = []
    for j in range(n_seq - 1):
        copy = to("seq", seq_to[j], mix_buf.at[seq], mix_buf.at[seq], mx_send.at[j], mx_recv.at[j])
        copy.start()
        mx_copies.append(copy)
    for copy in o_loads:
        copy.wait()

    columns = wo.shape[1]
    chunks = 4 if columns % 512 == 0 else 1
    chunk = columns // chunks

    def o_copy(c, r):
        index = c * n_head + r
        return to(
            "head", head_to[r], o_send.at[head_to[r], c], o_recv.at[r, c], os_sem.at[index], or_sem.at[index]
        )

    near = [
        sorted((o for o in range(n_seq) if o != s), key=lambda o: abs(o - s)) for s in range(n_seq)
    ]
    for j in range(n_seq):
        source = seq
        if j > 0:
            source = jnp.int32(0)
            for s in range(n_seq):
                source = jnp.where(seq == s, near[s][j - 1], source)
            slot = lax.rem(seq - source + n_seq - 1, n_seq)
            to("seq", source, mix_buf.at[source], mix_buf.at[source], mx_send.at[slot], mx_recv.at[slot]).wait_recv()
        last = j == n_seq - 1

        @pl.loop(0, chunks)
        def _(c):
            cols = pl.ds(pl.multiple_of(c * chunk, 128), chunk)
            value = jnp.dot(mix_buf[source], wo_buf[source, :, cols], preferred_element_type=f32)
            if j > 0:
                value = o_acc[:, cols] + value
            if not last:
                o_acc[:, cols] = value
                return
            for r in range(n_head):
                o_own[r, :, cols] = value[r * rows : (r + 1) * rows]
                o_send[r, c] = value[r * rows : (r + 1) * rows].astype(bf16)
            for r in range(n_head - 1):
                o_copy(c, r).start()

    for c in range(chunks):
        cols = slice(c * chunk, (c + 1) * chunk)
        for r in range(n_head - 1):
            o_copy(c, r).wait_recv()
        total = o_own[hd, :, cols]
        for r in range(n_head - 1):
            total = total + o_recv[r, c].astype(f32)
        out[:, cols] = total.astype(bf16)
    for copy in hid_copies + rs_copies + sq_copies + ag_copies + nk_copies + st_copies + ra_copies + mx_copies:
        copy.wait_send()
    for c in range(chunks):
        for r in range(n_head - 1):
            o_copy(c, r).wait_send()


def fused(n_seq, n_head, hidden, norm_gain, w_query, w_key, w_value, w_out, lengths, key_cache, value_cache):
    rows, feat = hidden.shape
    batch, kv, block, size = key_cache.shape
    heads = w_query.shape[1] // size
    own = heads // n_seq
    width = own * size
    columns = w_out.shape[1]
    chunks = 4 if columns % 512 == 0 else 1
    f32, bf16 = jnp.float32, jnp.bfloat16
    hbm = pl.BlockSpec(memory_space=pl.ANY)
    vmem = pl.BlockSpec(memory_space=pltpu.VMEM)
    smem = pl.BlockSpec(memory_space=pltpu.SMEM)
    dma = pltpu.SemaphoreType.DMA
    steps = [dma((n_seq,)), dma((n_seq,))]
    return pl.pallas_call(
        functools.partial(layer_kernel, n_seq, n_head),
        out_shape=jax.ShapeDtypeStruct((rows, columns), bf16),
        in_specs=[hbm, vmem, smem] + [hbm] * 6,
        out_specs=vmem,
        scratch_shapes=[
            pltpu.VMEM((n_head, rows, feat), bf16),
            pltpu.VMEM((batch, feat), f32),
            pltpu.VMEM((batch, feat), bf16),
            pltpu.VMEM((batch, block), jnp.int32),
            pltpu.VMEM((n_seq, feat, width), bf16),
            pltpu.VMEM((feat, 2 * kv * size), bf16),
            pltpu.VMEM((n_seq, width, columns), bf16),
            pltpu.VMEM(key_cache.shape, bf16),
            pltpu.VMEM(value_cache.shape, bf16),
            pltpu.VMEM((n_seq, batch, width + size), f32),
            pltpu.VMEM((n_seq - 1, batch, width + size), f32),
            pltpu.VMEM((n_seq, batch, 128), f32),
            pltpu.VMEM((n_seq, batch, width), bf16),
            pltpu.VMEM((n_seq, batch, size), bf16),
            pltpu.VMEM((heads * batch, size), f32),
            pltpu.VMEM((heads * batch, block), f32),
            pltpu.VMEM((heads * batch, size), f32),
            pltpu.VMEM((n_seq, batch, 128), f32),
            pltpu.VMEM((n_seq - 1, own * batch, size), bf16),
            pltpu.VMEM((n_seq - 1, own * batch, size), bf16),
            pltpu.VMEM((n_seq, batch, width), bf16),
            pltpu.VMEM((batch, columns), f32),
            pltpu.VMEM((n_head, rows, columns), f32),
            pltpu.VMEM((n_head, chunks, rows, columns // chunks), bf16),
            pltpu.VMEM((n_head - 1, chunks, rows, columns // chunks), bf16),
            dma((5 + 2 * n_seq,)),
            dma((n_head,)),
            dma((n_head,)),
            *steps, *steps, *steps, *steps, *steps, *steps, *steps,
            dma((4 * n_head,)),
            dma((4 * n_head,)),
        ],
        compiler_params=pltpu.CompilerParams(
            collective_id=0, has_side_effects=True, vmem_limit_bytes=60 * 1024 * 1024
        ),
    )(hidden, norm_gain.reshape(1, feat), lengths, w_query, w_key, w_value, w_out, key_cache, value_cache)


def program(n_seq, n_head, *args):
    w_query, key_cache = args[2], args[7]
    batch, kv, block, size = key_cache.shape
    heads = w_query.shape[1] // size
    own = max(heads // n_seq, 1)
    fits = (
        own * n_seq == heads
        and (heads // kv) % own == 0
        and 2 * kv == n_seq
        and size == 128
        and block == 128
        and heads <= 64
        and batch % 8 == 0
    )
    return fused(n_seq, n_head, *args) if fits else local(*args)


def solution(mesh):
    return jax.shard_map(
        functools.partial(program, mesh.shape["seq"], mesh.shape["head"]),
        mesh=mesh,
        in_specs=(
            P(("parts", "head"), "seq"),
            P("seq"),
            P("seq", "head"),
            P("seq", "head"),
            P("seq", "head"),
            P("head", "seq"),
            P("parts"),
            P("parts", "head", "seq", None),
            P("parts", "head", "seq", None),
        ),
        out_specs=P(("parts", "head"), "seq"),
        check_vma=False,
    )
```

```python
import functools

import jax
import jax.numpy as jnp
from jax import lax
from jax.experimental import pallas as pl
from jax.experimental.pallas import tpu as pltpu
from jax.sharding import PartitionSpec as P

D = 12288


EPSILON = 1e-05


def joined(value, axis, join):
    pieces = jax.tree.map(lambda part: lax.all_gather(part, axis), value)
    head = jax.tree.map(lambda part: part[0], pieces)
    tail = jax.tree.map(lambda part: part[1:], pieces)
    subtotal, _ = lax.scan(lambda subtotal, slab: (join(subtotal, slab), None), head, tail)
    return subtotal


def join_parts(earlier, later):
    new_max = jnp.maximum(earlier[0], later[0])
    left_factor = jnp.exp(earlier[0] - new_max)
    right_factor = jnp.exp(later[0] - new_max)
    den_total = earlier[1] * left_factor + later[1] * right_factor
    acc_total = earlier[2] * left_factor[..., None] + later[2] * right_factor[..., None]
    return (new_max, den_total, acc_total)


def local(hidden, norm_gain, w_query, w_key, w_value, w_out, lengths, key_cache, value_cache):
    batch_size, kv_local, block_len, head_size = key_cache.shape
    group_size = w_query.shape[1] // (kv_local * head_size)
    token_rows = lax.all_gather(hidden, "head", axis=0, tiled=True)
    widened = token_rows.astype(jnp.float32)
    square_local = jnp.sum(widened * widened, axis=1)
    scaled = (widened * norm_gain).astype(jnp.bfloat16)
    query_part = jnp.dot(scaled, w_query, preferred_element_type=jnp.float32)
    key_part = jnp.dot(scaled, w_key, preferred_element_type=jnp.float32)
    value_part = jnp.dot(scaled, w_value, preferred_element_type=jnp.float32)
    query_factor = float(head_size) ** (-0.5)
    norm_total = lax.psum(square_local, "seq")
    query_sum, key_sum, value_sum = lax.psum((query_part, key_part, value_part), "seq")
    inverse_rms = lax.rsqrt(norm_total / D + EPSILON)[:, None]
    queries = (query_sum * inverse_rms * query_factor).astype(jnp.bfloat16)
    new_keys = (key_sum * inverse_rms).astype(jnp.bfloat16)
    new_values = (value_sum * inverse_rms).astype(jnp.bfloat16)
    grouped = queries.reshape(batch_size, kv_local, group_size, head_size)
    scores = jnp.einsum("bkgd,bkpd->bkgp", grouped, key_cache, preferred_element_type=jnp.float32)
    offset = lax.axis_index("seq") * block_len
    positions = offset + jnp.arange(block_len, dtype=jnp.int32)
    live_mask = (positions[None, :] < lengths[:, None])[:, None, None, :]
    block_max = jnp.max(jnp.where(live_mask, scores, -1e30), axis=-1)
    shifted = jnp.where(live_mask, scores - block_max[..., None], 0.0)
    weights = jnp.where(live_mask, jnp.exp(shifted), 0.0).astype(jnp.bfloat16)
    block_den = jnp.sum(weights.astype(jnp.float32), axis=-1)
    block_acc = jnp.einsum(
        "bkgp,bkpd->bkgd", weights, value_cache, preferred_element_type=jnp.float32
    )
    self_score = jnp.einsum(
        "oips,ois->oip",
        grouped,
        new_keys.reshape(batch_size, kv_local, head_size),
        preferred_element_type=jnp.float32,
    )
    global_max, den_merged, acc_merged = joined(
        (block_max, block_den, block_acc), "seq", join_parts
    )
    top_score = jnp.maximum(global_max, self_score)
    factors = jnp.exp(global_max - top_score)
    den_sum = den_merged * factors
    acc_sum = acc_merged * factors[..., None]
    own_weight = jnp.exp(self_score - top_score)
    denominator = den_sum + own_weight
    numerator = acc_sum + own_weight[..., None] * new_values.reshape(
        batch_size, kv_local, 1, head_size
    ).astype(jnp.float32)
    mixed = (
        (numerator / denominator[..., None])
        .astype(jnp.bfloat16)
        .reshape(batch_size, kv_local * group_size * head_size)
    )
    output = lax.psum_scatter(
        jnp.dot(mixed, w_out, preferred_element_type=jnp.float32),
        "head",
        scatter_dimension=0,
        tiled=True,
    )
    return output.astype(jnp.bfloat16)


MESH = pl.DeviceIdType.MESH


def layer_kernel(
    n_seq, n_head, hid, gain, lens, wq, wk, wv, wo, kc, vc, out,
    hid_buf, x_scr, xs_scr, len_scr, wq_buf, wkv_buf, wo_buf, kc_buf, vc_buf,
    part, rs_buf, kv_part, kv_buf, sq_buf, ag_buf, nk_buf, q_scr, sc_scr, acc_scr, st_buf, acc_send, ra_buf, mix_buf, o_acc, o_own, o_send, o_recv,
    load_sem, hid_send, hid_recv, rs_send, rs_recv, kv_send, kv_recv, sq_send, sq_recv, ag_send, ag_recv, nk_send, nk_recv,
    st_send, st_recv, ra_send, ra_recv, mx_send, mx_recv, os_sem, or_sem,
):
    f32, bf16 = jnp.float32, jnp.bfloat16
    seq, hd = lax.axis_index("seq"), lax.axis_index("head")
    rows, feat = hid.shape
    batch, kv, block, size = kc.shape
    heads = wq.shape[1] // size
    group = heads // kv
    own = heads // n_seq
    width = own * size
    kv_cols = kv * size

    def load(index, source, target):
        copy = pltpu.make_async_copy(source, target, load_sem.at[index])
        copy.start()
        return copy

    def to(axis, index, source, target, send, recv):
        return pltpu.make_async_remote_copy(
            src_ref=source, dst_ref=target, send_sem=send, recv_sem=recv,
            device_id={axis: index}, device_id_type=MESH,
        )

    seq_to = [lax.rem(seq + j + 1, n_seq) for j in range(n_seq)]
    seq_from = [lax.rem(seq + n_seq - j - 1, n_seq) for j in range(n_seq)]
    head_to = [lax.rem(hd + j + 1, n_head) for j in range(n_head)]

    own_hidden = load(0, hid, hid_buf.at[hd])
    barrier = pltpu.get_barrier_semaphore()
    for j in range(n_head - 1):
        pl.semaphore_signal(barrier, inc=1, device_id={"head": head_to[j]}, device_id_type=MESH)
    for j in range(n_seq - 1):
        pl.semaphore_signal(barrier, inc=1, device_id={"seq": seq_to[j]}, device_id_type=MESH)
    key_load = load(1, wk, wkv_buf.at[:, pl.ds(0, kv_cols)])
    value_load = load(2, wv, wkv_buf.at[:, pl.ds(kv_cols, kv_cols)])
    q_loads = [
        load(3 + j, wq.at[:, pl.ds(pl.multiple_of(seq_to[j] * width, width), width)], wq_buf.at[j])
        for j in range(n_seq)
    ]
    base = 3 + n_seq
    kc_load = load(base, kc, kc_buf)
    vc_load = load(base + 1, vc, vc_buf)
    o_loads = [
        load(base + 2 + j, wo.at[pl.ds(j * width, width)], wo_buf.at[j]) for j in range(n_seq)
    ]

    own_hidden.wait()
    pl.semaphore_wait(barrier, n_head + n_seq - 2)

    hid_copies = [
        to("head", head_to[j], hid_buf.at[hd], hid_buf.at[hd], hid_send.at[j], hid_recv.at[j])
        for j in range(n_head - 1)
    ]
    for copy in hid_copies:
        copy.start()
    for b in range(batch):
        len_scr[b : b + 1, :] = jnp.full((1, block), lens[b], jnp.int32)
    for copy in hid_copies:
        copy.wait_recv()
    for j in range(n_head):
        x_scr[j * rows : (j + 1) * rows, :] = hid_buf[j].astype(f32)
    widened = x_scr[...]
    square = jnp.sum(widened * widened, axis=1, keepdims=True)
    sq_buf[n_seq - 1] = jnp.broadcast_to(square, (batch, 128))
    sq_copies = []
    for j in range(n_seq - 1):
        copy = to("seq", seq_to[j], sq_buf.at[n_seq - 1], sq_buf.at[j], sq_send.at[j], sq_recv.at[j])
        copy.start()
        sq_copies.append(copy)
    xs_scr[...] = (widened * gain[...]).astype(bf16)

    tile = 256 if width % 256 == 0 else size
    pieces = width // tile
    rs_copies = []
    for j in range(n_seq):
        q_loads[j].wait()
        for n in range(pieces):
            cols = slice(n * tile, (n + 1) * tile)
            part[j, n] = jnp.dot(xs_scr[...], wq_buf[j, :, cols], preferred_element_type=f32)
            if j < n_seq - 1:
                index = j * pieces + n
                copy = to(
                    "seq", seq_to[j], part.at[j, n], rs_buf.at[j, n], rs_send.at[index], rs_recv.at[index]
                )
                copy.start()
                rs_copies.append(copy)
    key_load.wait()
    value_load.wait()
    for j in range(n_seq):
        kv_at = pl.ds(pl.multiple_of(seq_to[j] * size, size), size)
        kv_part[j] = jnp.dot(xs_scr[...], wkv_buf[:, kv_at], preferred_element_type=f32)

    for copy in sq_copies:
        copy.wait_recv()
    square_sum = sq_buf[0]
    for j in range(1, n_seq):
        square_sum = square_sum + sq_buf[j]
    mean_square = square_sum / (feat * n_seq)
    inverse_rms = lax.rsqrt(mean_square + EPSILON)[:, :1]
    factor = float(size) ** (-0.5)
    for n in range(pieces):
        total = part[n_seq - 1, n]
        for j in range(n_seq - 1):
            rs_copies[j * pieces + n].wait_recv()
            total = total + rs_buf[j, n]
        ag_buf[seq, :, n * tile : (n + 1) * tile] = (total * inverse_rms * factor).astype(bf16)
    ag_copies = []
    for j in range(n_seq - 1):
        copy = to("seq", seq_to[j], ag_buf.at[seq], ag_buf.at[seq], ag_send.at[j], ag_recv.at[j])
        copy.start()
        ag_copies.append(copy)
    kv_copies = []
    for j in range(n_seq - 1):
        copy = to("seq", seq_to[j], kv_part.at[j], kv_buf.at[j], kv_send.at[j], kv_recv.at[j])
        copy.start()
        kv_copies.append(copy)
    kc_load.wait()
    vc_load.wait()
    unroll = 6 if batch % 6 == 0 else 1
    sources = n_seq // kv

    def take_queries(source, remote):
        if remote:
            slot = lax.rem(seq - source + n_seq - 1, n_seq)
            to("seq", source, ag_buf.at[source], ag_buf.at[source], ag_send.at[slot], ag_recv.at[slot]).wait_recv()
        for i in range(own):
            at = pl.multiple_of((source * own + i) * batch, 8)
            q_scr[pl.ds(at, batch), :] = ag_buf[source, :, i * size : (i + 1) * size].astype(f32)

    def score(k):
        @pl.loop(0, batch // unroll)
        def _(step):
            for u in range(unroll):
                b = step * unroll + u
                at = pl.ds(k * group * batch + b, group, stride=batch)
                sc_scr[at, :] = lax.dot_general(
                    q_scr[at, :].astype(bf16), kc_buf[b, k], (((1,), (1,)), ((), ())),
                    preferred_element_type=f32,
                )

    def accumulate(k):
        @pl.loop(0, batch // unroll)
        def _(step):
            for u in range(unroll):
                b = step * unroll + u
                at = pl.ds(k * group * batch + b, group, stride=batch)
                acc_scr[at, :] = jnp.dot(
                    sc_scr[at, :].astype(bf16), vc_buf[b, k], preferred_element_type=f32
                )

    lane = lax.broadcasted_iota(jnp.int32, (batch, block), 1)
    live = lane + seq * block < len_scr[...]

    def soften(k, stats):
        for g in range(group):
            h = k * group + g
            at = pl.ds(pl.multiple_of(h * batch, 8), batch)
            scores = sc_scr[at, :]
            top = jnp.max(jnp.where(live, scores, -1e30), axis=1, keepdims=True)
            shifted = jnp.where(live, scores - top, 0.0)
            weights = jnp.where(live, jnp.exp(shifted), 0.0).astype(bf16).astype(f32)
            sc_scr[at, :] = weights
            total = jnp.sum(weights, axis=1, keepdims=True)
            stats = jnp.where(lane == h, top, jnp.where(lane == 64 + h, total, stats))
        return stats

    kv_head = (seq * own) // group
    stats = jnp.zeros((batch, 128), f32)
    take_queries(seq, False)
    for t in range(1, sources):
        take_queries(kv_head * sources + lax.rem(seq + t, sources), True)
    score(kv_head)
    stats = soften(kv_head, stats)
    if kv > 1:
        accumulate(kv_head)
    others = [lax.rem(kv_head + t, kv) for t in range(1, kv)]
    for k in others:
        for t in range(sources):
            take_queries(k * sources + t, True)
        score(k)
        stats = soften(k, stats)
    st_buf[n_seq - 1] = stats
    st_copies = []
    for j in range(n_seq - 1):
        copy = to("seq", seq_to[j], st_buf.at[n_seq - 1], st_buf.at[j], st_send.at[j], st_recv.at[j])
        copy.start()
        st_copies.append(copy)
    new_part = kv_part[n_seq - 1]
    for j in range(n_seq - 1):
        kv_copies[j].wait_recv()
        new_part = new_part + kv_buf[j]
    nk_buf[seq] = (new_part * inverse_rms).astype(bf16)
    nk_copies = []
    for j in range(n_seq - 1):
        copy = to("seq", seq_to[j], nk_buf.at[seq], nk_buf.at[seq], nk_send.at[j], nk_recv.at[j])
        copy.start()
        nk_copies.append(copy)
    for k in others if kv > 1 else [kv_head]:
        accumulate(k)

    ra_copies = []
    part_rows = own * batch
    for j in range(n_seq - 1):
        at = pl.ds(pl.multiple_of(seq_to[j] * part_rows, part_rows), part_rows)
        acc_send[j] = acc_scr[at, :].astype(bf16)
        copy = to("seq", seq_to[j], acc_send.at[j], ra_buf.at[j], ra_send.at[j], ra_recv.at[j])
        copy.start()
        ra_copies.append(copy)

    for copy in nk_copies:
        copy.wait_recv()
    new_key = nk_buf[kv_head].astype(f32)
    new_value = nk_buf[kv + kv_head].astype(f32)
    own_at = pl.multiple_of(seq * part_rows, part_rows)
    self_score = jnp.zeros((batch, 128), f32)
    for i in range(own):
        query = q_scr[pl.ds(own_at + i * batch, batch), :]
        score = jnp.sum(query * new_key, axis=1, keepdims=True)
        self_score = jnp.where(lane == i, score, self_score)
    for copy in st_copies:
        copy.wait_recv()
    shift = lax.rem(128 - seq * own, 128)
    maxes = [pltpu.roll(st_buf[j], shift, 1) for j in range(n_seq)]
    dens = [pltpu.roll(m, 64, 1) for m in maxes]
    top_score = self_score
    for m in maxes:
        top_score = jnp.maximum(top_score, m)
    factors = [jnp.exp(m - top_score) for m in maxes]
    own_weight = jnp.exp(self_score - top_score)
    denominator = own_weight
    for f, d in zip(factors, dens):
        denominator = denominator + f * d
    own_weight = own_weight / denominator
    factors = [f / denominator for f in factors]
    for copy in ra_copies:
        copy.wait_recv()
    for i in range(own):
        mixed = own_weight[:, i : i + 1] * new_value
        mixed += factors[n_seq - 1][:, i : i + 1] * acc_scr[pl.ds(own_at + i * batch, batch), :]
        for j in range(n_seq - 1):
            mixed += factors[j][:, i : i + 1] * ra_buf[j, i * batch : (i + 1) * batch, :].astype(f32)
        mix_buf[seq, :, i * size : (i + 1) * size] = mixed.astype(bf16)
    mx_copies = []
    for j in range(n_seq - 1):
        copy = to("seq", seq_to[j], mix_buf.at[seq], mix_buf.at[seq], mx_send.at[j], mx_recv.at[j])
        copy.start()
        mx_copies.append(copy)
    for copy in o_loads:
        copy.wait()

    columns = wo.shape[1]
    chunks = 4 if columns % 512 == 0 else 1
    chunk = columns // chunks

    def o_copy(c, r):
        index = c * n_head + r
        return to(
            "head", head_to[r], o_send.at[head_to[r], c], o_recv.at[r, c], os_sem.at[index], or_sem.at[index]
        )

    near = [
        sorted((o for o in range(n_seq) if o != s), key=lambda o: abs(o - s)) for s in range(n_seq)
    ]
    for j in range(n_seq):
        source = seq
        if j > 0:
            source = jnp.int32(0)
            for s in range(n_seq):
                source = jnp.where(seq == s, near[s][j - 1], source)
            slot = lax.rem(seq - source + n_seq - 1, n_seq)
            to("seq", source, mix_buf.at[source], mix_buf.at[source], mx_send.at[slot], mx_recv.at[slot]).wait_recv()
        last = j == n_seq - 1

        @pl.loop(0, chunks)
        def _(c):
            cols = pl.ds(pl.multiple_of(c * chunk, 128), chunk)
            value = jnp.dot(mix_buf[source], wo_buf[source, :, cols], preferred_element_type=f32)
            if j > 0:
                value = o_acc[:, cols] + value
            if not last:
                o_acc[:, cols] = value
                return
            for r in range(n_head):
                o_own[r, :, cols] = value[r * rows : (r + 1) * rows]
                o_send[r, c] = value[r * rows : (r + 1) * rows].astype(bf16)
            for r in range(n_head - 1):
                o_copy(c, r).start()

    for c in range(chunks):
        cols = slice(c * chunk, (c + 1) * chunk)
        for r in range(n_head - 1):
            o_copy(c, r).wait_recv()
        total = o_own[hd, :, cols]
        for r in range(n_head - 1):
            total = total + o_recv[r, c].astype(f32)
        out[:, cols] = total.astype(bf16)
    for copy in hid_copies + rs_copies + kv_copies + sq_copies + ag_copies + nk_copies + st_copies + ra_copies + mx_copies:
        copy.wait_send()
    for c in range(chunks):
        for r in range(n_head - 1):
            o_copy(c, r).wait_send()


def fused(n_seq, n_head, hidden, norm_gain, w_query, w_key, w_value, w_out, lengths, key_cache, value_cache):
    rows, feat = hidden.shape
    batch, kv, block, size = key_cache.shape
    heads = w_query.shape[1] // size
    own = heads // n_seq
    width = own * size
    tile = 256 if width % 256 == 0 else size
    columns = w_out.shape[1]
    chunks = 4 if columns % 512 == 0 else 1
    f32, bf16 = jnp.float32, jnp.bfloat16
    hbm = pl.BlockSpec(memory_space=pl.ANY)
    vmem = pl.BlockSpec(memory_space=pltpu.VMEM)
    smem = pl.BlockSpec(memory_space=pltpu.SMEM)
    dma = pltpu.SemaphoreType.DMA
    steps = [dma((n_seq,)), dma((n_seq,))]
    return pl.pallas_call(
        functools.partial(layer_kernel, n_seq, n_head),
        out_shape=jax.ShapeDtypeStruct((rows, columns), bf16),
        in_specs=[hbm, vmem, smem] + [hbm] * 6,
        out_specs=vmem,
        scratch_shapes=[
            pltpu.VMEM((n_head, rows, feat), bf16),
            pltpu.VMEM((batch, feat), f32),
            pltpu.VMEM((batch, feat), bf16),
            pltpu.VMEM((batch, block), jnp.int32),
            pltpu.VMEM((n_seq, feat, width), bf16),
            pltpu.VMEM((feat, 2 * kv * size), bf16),
            pltpu.VMEM((n_seq, width, columns), bf16),
            pltpu.VMEM(key_cache.shape, bf16),
            pltpu.VMEM(value_cache.shape, bf16),
            pltpu.VMEM((n_seq, width // tile, batch, tile), f32),
            pltpu.VMEM((n_seq - 1, width // tile, batch, tile), f32),
            pltpu.VMEM((n_seq, batch, size), f32),
            pltpu.VMEM((n_seq - 1, batch, size), f32),
            pltpu.VMEM((n_seq, batch, 128), f32),
            pltpu.VMEM((n_seq, batch, width), bf16),
            pltpu.VMEM((n_seq, batch, size), bf16),
            pltpu.VMEM((heads * batch, size), f32),
            pltpu.VMEM((heads * batch, block), f32),
            pltpu.VMEM((heads * batch, size), f32),
            pltpu.VMEM((n_seq, batch, 128), f32),
            pltpu.VMEM((n_seq - 1, own * batch, size), bf16),
            pltpu.VMEM((n_seq - 1, own * batch, size), bf16),
            pltpu.VMEM((n_seq, batch, width), bf16),
            pltpu.VMEM((batch, columns), f32),
            pltpu.VMEM((n_head, rows, columns), f32),
            pltpu.VMEM((n_head, chunks, rows, columns // chunks), bf16),
            pltpu.VMEM((n_head - 1, chunks, rows, columns // chunks), bf16),
            dma((5 + 2 * n_seq,)),
            dma((n_head,)),
            dma((n_head,)),
            dma((n_seq * width // tile,)),
            dma((n_seq * width // tile,)),
            *steps, *steps, *steps, *steps, *steps, *steps, *steps,
            dma((4 * n_head,)),
            dma((4 * n_head,)),
        ],
        compiler_params=pltpu.CompilerParams(
            collective_id=0, has_side_effects=True, vmem_limit_bytes=60 * 1024 * 1024
        ),
    )(hidden, norm_gain.reshape(1, feat), lengths, w_query, w_key, w_value, w_out, key_cache, value_cache)


def program(n_seq, n_head, *args):
    w_query, key_cache = args[2], args[7]
    batch, kv, block, size = key_cache.shape
    heads = w_query.shape[1] // size
    own = max(heads // n_seq, 1)
    fits = (
        own * n_seq == heads
        and (heads // kv) % own == 0
        and 2 * kv == n_seq
        and size == 128
        and block == 128
        and heads <= 64
        and batch % 8 == 0
    )
    return fused(n_seq, n_head, *args) if fits else local(*args)


def solution(mesh):
    return jax.shard_map(
        functools.partial(program, mesh.shape["seq"], mesh.shape["head"]),
        mesh=mesh,
        in_specs=(
            P(("parts", "head"), "seq"),
            P("seq"),
            P("seq", "head"),
            P("seq", "head"),
            P("seq", "head"),
            P("head", "seq"),
            P("parts"),
            P("parts", "head", "seq", None),
            P("parts", "head", "seq", None),
        ),
        out_specs=P(("parts", "head"), "seq"),
        check_vma=False,
    )
```

```python
import functools

import jax
import jax.numpy as jnp
from jax import lax
from jax.experimental import pallas as pl
from jax.experimental.pallas import tpu as pltpu
from jax.sharding import PartitionSpec as P

D = 12288


EPSILON = 1e-05


def joined(value, axis, join):
    pieces = jax.tree.map(lambda part: lax.all_gather(part, axis), value)
    head = jax.tree.map(lambda part: part[0], pieces)
    tail = jax.tree.map(lambda part: part[1:], pieces)
    subtotal, _ = lax.scan(lambda subtotal, slab: (join(subtotal, slab), None), head, tail)
    return subtotal


def join_parts(earlier, later):
    new_max = jnp.maximum(earlier[0], later[0])
    left_factor = jnp.exp(earlier[0] - new_max)
    right_factor = jnp.exp(later[0] - new_max)
    den_total = earlier[1] * left_factor + later[1] * right_factor
    acc_total = earlier[2] * left_factor[..., None] + later[2] * right_factor[..., None]
    return (new_max, den_total, acc_total)


def local(hidden, norm_gain, w_query, w_key, w_value, w_out, lengths, key_cache, value_cache):
    batch_size, kv_local, block_len, head_size = key_cache.shape
    group_size = w_query.shape[1] // (kv_local * head_size)
    token_rows = lax.all_gather(hidden, "head", axis=0, tiled=True)
    widened = token_rows.astype(jnp.float32)
    square_local = jnp.sum(widened * widened, axis=1)
    scaled = (widened * norm_gain).astype(jnp.bfloat16)
    query_part = jnp.dot(scaled, w_query, preferred_element_type=jnp.float32)
    key_part = jnp.dot(scaled, w_key, preferred_element_type=jnp.float32)
    value_part = jnp.dot(scaled, w_value, preferred_element_type=jnp.float32)
    query_factor = float(head_size) ** (-0.5)
    norm_total = lax.psum(square_local, "seq")
    query_sum, key_sum, value_sum = lax.psum((query_part, key_part, value_part), "seq")
    inverse_rms = lax.rsqrt(norm_total / D + EPSILON)[:, None]
    queries = (query_sum * inverse_rms * query_factor).astype(jnp.bfloat16)
    new_keys = (key_sum * inverse_rms).astype(jnp.bfloat16)
    new_values = (value_sum * inverse_rms).astype(jnp.bfloat16)
    grouped = queries.reshape(batch_size, kv_local, group_size, head_size)
    scores = jnp.einsum("bkgd,bkpd->bkgp", grouped, key_cache, preferred_element_type=jnp.float32)
    offset = lax.axis_index("seq") * block_len
    positions = offset + jnp.arange(block_len, dtype=jnp.int32)
    live_mask = (positions[None, :] < lengths[:, None])[:, None, None, :]
    block_max = jnp.max(jnp.where(live_mask, scores, -1e30), axis=-1)
    shifted = jnp.where(live_mask, scores - block_max[..., None], 0.0)
    weights = jnp.where(live_mask, jnp.exp(shifted), 0.0).astype(jnp.bfloat16)
    block_den = jnp.sum(weights.astype(jnp.float32), axis=-1)
    block_acc = jnp.einsum(
        "bkgp,bkpd->bkgd", weights, value_cache, preferred_element_type=jnp.float32
    )
    self_score = jnp.einsum(
        "oips,ois->oip",
        grouped,
        new_keys.reshape(batch_size, kv_local, head_size),
        preferred_element_type=jnp.float32,
    )
    global_max, den_merged, acc_merged = joined(
        (block_max, block_den, block_acc), "seq", join_parts
    )
    top_score = jnp.maximum(global_max, self_score)
    factors = jnp.exp(global_max - top_score)
    den_sum = den_merged * factors
    acc_sum = acc_merged * factors[..., None]
    own_weight = jnp.exp(self_score - top_score)
    denominator = den_sum + own_weight
    numerator = acc_sum + own_weight[..., None] * new_values.reshape(
        batch_size, kv_local, 1, head_size
    ).astype(jnp.float32)
    mixed = (
        (numerator / denominator[..., None])
        .astype(jnp.bfloat16)
        .reshape(batch_size, kv_local * group_size * head_size)
    )
    output = lax.psum_scatter(
        jnp.dot(mixed, w_out, preferred_element_type=jnp.float32),
        "head",
        scatter_dimension=0,
        tiled=True,
    )
    return output.astype(jnp.bfloat16)


MESH = pl.DeviceIdType.MESH


def layer_kernel(
    n_seq, n_head, hid, gain, lens, wq, wk, wv, wo, kc, vc, out,
    hid_buf, x_scr, xs_scr, len_scr, wq_buf, wkv_buf, wo_buf, kc_buf, vc_buf,
    part, rs_buf, kv_part, kv_buf, sq_buf, ag_buf, nk_buf, q_scr, sc_scr, acc_scr, st_buf, acc_send, ra_buf, mix_buf, o_acc, o_own, o_send, o_recv,
    load_sem, hid_send, hid_recv, rs_send, rs_recv, kv_send, kv_recv, sq_send, sq_recv, ag_send, ag_recv, nk_send, nk_recv,
    st_send, st_recv, ra_send, ra_recv, mx_send, mx_recv, os_sem, or_sem,
):
    f32, bf16 = jnp.float32, jnp.bfloat16
    seq, hd = lax.axis_index("seq"), lax.axis_index("head")
    rows, feat = hid.shape
    batch, kv, block, size = kc.shape
    heads = wq.shape[1] // size
    group = heads // kv
    own = heads // n_seq
    width = own * size
    kv_cols = kv * size

    def load(index, source, target):
        copy = pltpu.make_async_copy(source, target, load_sem.at[index])
        copy.start()
        return copy

    def to(axis, index, source, target, send, recv):
        return pltpu.make_async_remote_copy(
            src_ref=source, dst_ref=target, send_sem=send, recv_sem=recv,
            device_id={axis: index}, device_id_type=MESH,
        )

    near = [
        sorted((o for o in range(n_seq) if o != s), key=lambda o: abs(o - s)) for s in range(n_seq)
    ]

    def nearest(j):
        device = jnp.int32(0)
        for s in range(n_seq):
            device = jnp.where(seq == s, near[s][j], device)
        return device

    seq_to = [nearest(n_seq - 2 - j) for j in range(n_seq - 1)] + [seq]
    slots = [lax.rem(seq_to[j] - seq + n_seq - 1, n_seq) for j in range(n_seq - 1)]
    tile = 256 if width % 256 == 0 else size
    pieces = width // tile
    head_to = [lax.rem(hd + j + 1, n_head) for j in range(n_head)]

    own_hidden = load(0, hid, hid_buf.at[hd])
    barrier = pltpu.get_barrier_semaphore()
    for j in range(n_head - 1):
        pl.semaphore_signal(barrier, inc=1, device_id={"head": head_to[j]}, device_id_type=MESH)
    for j in range(n_seq - 1):
        pl.semaphore_signal(barrier, inc=1, device_id={"seq": seq_to[j]}, device_id_type=MESH)
    q_loads = [
        load(
            3 + n * n_seq + j,
            wq.at[:, pl.ds(pl.multiple_of(seq_to[j] * width + n * tile, tile), tile)],
            wq_buf.at[n * n_seq + j],
        )
        for n in range(pieces) for j in range(n_seq)
    ]
    key_load = load(1, wk, wkv_buf.at[:, pl.ds(0, kv_cols)])
    value_load = load(2, wv, wkv_buf.at[:, pl.ds(kv_cols, kv_cols)])
    base = 3 + n_seq * pieces
    kc_load = load(base, kc, kc_buf)
    vc_load = load(base + 1, vc, vc_buf)
    o_loads = [
        load(base + 2 + j, wo.at[pl.ds(j * width, width)], wo_buf.at[j]) for j in range(n_seq)
    ]

    own_hidden.wait()
    pl.semaphore_wait(barrier, n_head + n_seq - 2)

    hid_copies = [
        to("head", head_to[j], hid_buf.at[hd], hid_buf.at[hd], hid_send.at[j], hid_recv.at[j])
        for j in range(n_head - 1)
    ]
    for copy in hid_copies:
        copy.start()
    for b in range(batch):
        len_scr[b : b + 1, :] = jnp.full((1, block), lens[b], jnp.int32)
    for copy in hid_copies:
        copy.wait_recv()
    for j in range(n_head):
        x_scr[j * rows : (j + 1) * rows, :] = hid_buf[j].astype(f32)
    widened = x_scr[...]
    square = jnp.sum(widened * widened, axis=1, keepdims=True)
    sq_buf[n_seq - 1] = jnp.broadcast_to(square, (batch, 128))
    sq_copies = []
    for j in range(n_seq - 1):
        copy = to("seq", seq_to[j], sq_buf.at[n_seq - 1], sq_buf.at[slots[j]], sq_send.at[j], sq_recv.at[slots[j]])
        copy.start()
        sq_copies.append(copy)
    xs_scr[...] = (widened * gain[...]).astype(bf16)

    rs_copies = []
    for n in range(pieces):
        for j in range(n_seq):
            q_loads[n * n_seq + j].wait()
            part[j, n] = jnp.dot(xs_scr[...], wq_buf[n * n_seq + j], preferred_element_type=f32)
            if j < n_seq - 1:
                copy = to(
                    "seq", seq_to[j], part.at[j, n], rs_buf.at[slots[j], n],
                    rs_send.at[j * pieces + n], rs_recv.at[slots[j] * pieces + n],
                )
                copy.start()
                rs_copies.append(copy)
    key_load.wait()
    value_load.wait()
    for j in range(n_seq):
        kv_at = pl.ds(pl.multiple_of(seq_to[j] * size, size), size)
        kv_part[j] = jnp.dot(xs_scr[...], wkv_buf[:, kv_at], preferred_element_type=f32)

    for copy in sq_copies:
        copy.wait_recv()
    square_sum = sq_buf[0]
    for j in range(1, n_seq):
        square_sum = square_sum + sq_buf[j]
    mean_square = square_sum / (feat * n_seq)
    inverse_rms = lax.rsqrt(mean_square + EPSILON)[:, :1]
    factor = float(size) ** (-0.5)
    ag_copies = []
    for n in range(pieces):
        for j in range(n_seq - 1):
            rs_copies[n * (n_seq - 1) + j].wait_recv()
        total = part[n_seq - 1, n]
        for j in range(n_seq - 1):
            total = total + rs_buf[j, n]
        ag_buf[seq, n] = (total * inverse_rms * factor).astype(bf16)
        for j in range(n_seq - 1):
            copy = to(
                "seq", seq_to[j], ag_buf.at[seq, n], ag_buf.at[seq, n],
                ag_send.at[j * pieces + n], ag_recv.at[slots[j] * pieces + n],
            )
            copy.start()
            ag_copies.append(copy)
    kv_copies = []
    for j in range(n_seq - 1):
        copy = to("seq", seq_to[j], kv_part.at[j], kv_buf.at[slots[j]], kv_send.at[j], kv_recv.at[slots[j]])
        copy.start()
        kv_copies.append(copy)
    kc_load.wait()
    vc_load.wait()
    unroll = 6 if batch % 6 == 0 else 1
    sources = n_seq // kv

    def take_queries(source, remote):
        if remote:
            slot = lax.rem(seq - source + n_seq - 1, n_seq)
            for n in range(pieces):
                index = slot * pieces + n
                to(
                    "seq", source, ag_buf.at[source, n], ag_buf.at[source, n], ag_send.at[index], ag_recv.at[index]
                ).wait_recv()
        for i in range(own):
            at = pl.multiple_of((source * own + i) * batch, 8)
            n, first = divmod(i * size, tile)
            q_scr[pl.ds(at, batch), :] = ag_buf[source, n, :, first : first + size].astype(f32)

    def score(k):
        @pl.loop(0, batch // unroll)
        def _(step):
            for u in range(unroll):
                b = step * unroll + u
                at = pl.ds(k * group * batch + b, group, stride=batch)
                sc_scr[at, :] = lax.dot_general(
                    q_scr[at, :].astype(bf16), kc_buf[b, k], (((1,), (1,)), ((), ())),
                    preferred_element_type=f32,
                )

    def accumulate(k):
        @pl.loop(0, batch // unroll)
        def _(step):
            for u in range(unroll):
                b = step * unroll + u
                at = pl.ds(k * group * batch + b, group, stride=batch)
                acc_scr[at, :] = jnp.dot(
                    sc_scr[at, :].astype(bf16), vc_buf[b, k], preferred_element_type=f32
                )

    lane = lax.broadcasted_iota(jnp.int32, (batch, block), 1)
    live = lane + seq * block < len_scr[...]

    def soften(k, stats):
        for g in range(group):
            h = k * group + g
            at = pl.ds(pl.multiple_of(h * batch, 8), batch)
            scores = sc_scr[at, :]
            top = jnp.max(jnp.where(live, scores, -1e30), axis=1, keepdims=True)
            shifted = jnp.where(live, scores - top, 0.0)
            weights = jnp.where(live, jnp.exp(shifted), 0.0).astype(bf16).astype(f32)
            sc_scr[at, :] = weights
            total = jnp.sum(weights, axis=1, keepdims=True)
            stats = jnp.where(lane == h, top, jnp.where(lane == 64 + h, total, stats))
        return stats

    kv_head = (seq * own) // group
    stats = jnp.zeros((batch, 128), f32)
    take_queries(seq, False)
    for t in range(1, sources):
        take_queries(kv_head * sources + lax.rem(seq + t, sources), True)
    score(kv_head)
    stats = soften(kv_head, stats)
    if kv > 1:
        accumulate(kv_head)
    others = [lax.rem(kv_head + t, kv) for t in range(1, kv)]
    for k in others:
        for t in range(sources):
            take_queries(k * sources + t, True)
        score(k)
        stats = soften(k, stats)
    st_buf[n_seq - 1] = stats
    st_copies = []
    for j in range(n_seq - 1):
        copy = to("seq", seq_to[j], st_buf.at[n_seq - 1], st_buf.at[slots[j]], st_send.at[j], st_recv.at[slots[j]])
        copy.start()
        st_copies.append(copy)
    new_part = kv_part[n_seq - 1]
    for copy in kv_copies:
        copy.wait_recv()
    for j in range(n_seq - 1):
        new_part = new_part + kv_buf[j]
    nk_buf[seq] = (new_part * inverse_rms).astype(bf16)
    nk_copies = []
    for j in range(n_seq - 1):
        copy = to("seq", seq_to[j], nk_buf.at[seq], nk_buf.at[seq], nk_send.at[j], nk_recv.at[slots[j]])
        copy.start()
        nk_copies.append(copy)
    for k in others if kv > 1 else [kv_head]:
        accumulate(k)

    ra_copies = []
    part_rows = own * batch
    for j in range(n_seq - 1):
        at = pl.ds(pl.multiple_of(seq_to[j] * part_rows, part_rows), part_rows)
        acc_send[j] = acc_scr[at, :].astype(bf16)
    piece_heads = tile // size
    piece_rows = piece_heads * batch
    for n in range(pieces):
        for j in range(n_seq - 1):
            copy = to(
                "seq", seq_to[j], acc_send.at[j, pl.ds(n * piece_rows, piece_rows)],
                ra_buf.at[slots[j], pl.ds(n * piece_rows, piece_rows)],
                ra_send.at[j * pieces + n], ra_recv.at[slots[j] * pieces + n],
            )
            copy.start()
            ra_copies.append(copy)

    for copy in nk_copies:
        copy.wait_recv()
    new_key = nk_buf[kv_head].astype(f32)
    new_value = nk_buf[kv + kv_head].astype(f32)
    own_at = pl.multiple_of(seq * part_rows, part_rows)
    self_score = jnp.zeros((batch, 128), f32)
    for i in range(own):
        query = q_scr[pl.ds(own_at + i * batch, batch), :]
        score = jnp.sum(query * new_key, axis=1, keepdims=True)
        self_score = jnp.where(lane == i, score, self_score)
    for copy in st_copies:
        copy.wait_recv()
    shift = lax.rem(128 - seq * own, 128)
    maxes = [pltpu.roll(st_buf[j], shift, 1) for j in range(n_seq)]
    dens = [pltpu.roll(m, 64, 1) for m in maxes]
    top_score = self_score
    for m in maxes:
        top_score = jnp.maximum(top_score, m)
    factors = [jnp.exp(m - top_score) for m in maxes]
    own_weight = jnp.exp(self_score - top_score)
    denominator = own_weight
    for f, d in zip(factors, dens):
        denominator = denominator + f * d
    own_weight = own_weight / denominator
    factors = [f / denominator for f in factors]
    mx_copies = []
    for n in range(pieces):
        for j in range(n_seq - 1):
            ra_copies[n * (n_seq - 1) + j].wait_recv()
        for p in range(piece_heads):
            i = n * piece_heads + p
            mixed = own_weight[:, i : i + 1] * new_value
            mixed += factors[n_seq - 1][:, i : i + 1] * acc_scr[pl.ds(own_at + i * batch, batch), :]
            for j in range(n_seq - 1):
                mixed += factors[j][:, i : i + 1] * ra_buf[j, i * batch : (i + 1) * batch, :].astype(f32)
            mix_buf[seq, n, :, p * size : (p + 1) * size] = mixed.astype(bf16)
        for j in range(n_seq - 1):
            copy = to(
                "seq", seq_to[j], mix_buf.at[seq, n], mix_buf.at[seq, n],
                mx_send.at[j * pieces + n], mx_recv.at[slots[j] * pieces + n],
            )
            copy.start()
            mx_copies.append(copy)
    for copy in o_loads:
        copy.wait()

    columns = wo.shape[1]
    chunks = 4 if columns % 512 == 0 else 1
    chunk = columns // chunks

    def mix_of(source):
        return jnp.concatenate([mix_buf[source, n] for n in range(pieces)], axis=1)

    def o_copy(c, r):
        index = c * n_head + r
        return to(
            "head", head_to[r], o_send.at[head_to[r], c], o_recv.at[r, c], os_sem.at[index], or_sem.at[index]
        )

    for j in range(n_seq):
        source = seq
        if j > 0:
            source = nearest(j - 1)
            slot = lax.rem(seq - source + n_seq - 1, n_seq)
            for n in range(pieces):
                index = slot * pieces + n
                to(
                    "seq", source, mix_buf.at[source, n], mix_buf.at[source, n], mx_send.at[index], mx_recv.at[index]
                ).wait_recv()
        last = j == n_seq - 1

        @pl.loop(0, chunks)
        def _(c):
            cols = pl.ds(pl.multiple_of(c * chunk, 128), chunk)
            value = jnp.dot(mix_of(source), wo_buf[source, :, cols], preferred_element_type=f32)
            if j > 0:
                value = o_acc[:, cols] + value
            if not last:
                o_acc[:, cols] = value
                return
            for r in range(n_head):
                o_own[r, :, cols] = value[r * rows : (r + 1) * rows]
                o_send[r, c] = value[r * rows : (r + 1) * rows].astype(bf16)
            for r in range(n_head - 1):
                o_copy(c, r).start()

    for c in range(chunks):
        cols = slice(c * chunk, (c + 1) * chunk)
        for r in range(n_head - 1):
            o_copy(c, r).wait_recv()
        total = o_own[hd, :, cols]
        for r in range(n_head - 1):
            total = total + o_recv[r, c].astype(f32)
        out[:, cols] = total.astype(bf16)
    for copy in hid_copies + rs_copies + kv_copies + sq_copies + ag_copies + nk_copies + st_copies + ra_copies + mx_copies:
        copy.wait_send()
    for c in range(chunks):
        for r in range(n_head - 1):
            o_copy(c, r).wait_send()


def fused(n_seq, n_head, hidden, norm_gain, w_query, w_key, w_value, w_out, lengths, key_cache, value_cache):
    rows, feat = hidden.shape
    batch, kv, block, size = key_cache.shape
    heads = w_query.shape[1] // size
    own = heads // n_seq
    width = own * size
    tile = 256 if width % 256 == 0 else size
    columns = w_out.shape[1]
    chunks = 4 if columns % 512 == 0 else 1
    f32, bf16 = jnp.float32, jnp.bfloat16
    hbm = pl.BlockSpec(memory_space=pl.ANY)
    vmem = pl.BlockSpec(memory_space=pltpu.VMEM)
    smem = pl.BlockSpec(memory_space=pltpu.SMEM)
    dma = pltpu.SemaphoreType.DMA
    steps = [dma((n_seq,)), dma((n_seq,))]
    many = [dma((n_seq * width // tile,)), dma((n_seq * width // tile,))]
    return pl.pallas_call(
        functools.partial(layer_kernel, n_seq, n_head),
        out_shape=jax.ShapeDtypeStruct((rows, columns), bf16),
        in_specs=[hbm, vmem, smem] + [hbm] * 6,
        out_specs=vmem,
        scratch_shapes=[
            pltpu.VMEM((n_head, rows, feat), bf16),
            pltpu.VMEM((batch, feat), f32),
            pltpu.VMEM((batch, feat), bf16),
            pltpu.VMEM((batch, block), jnp.int32),
            pltpu.VMEM((n_seq * width // tile, feat, tile), bf16),
            pltpu.VMEM((feat, 2 * kv * size), bf16),
            pltpu.VMEM((n_seq, width, columns), bf16),
            pltpu.VMEM(key_cache.shape, bf16),
            pltpu.VMEM(value_cache.shape, bf16),
            pltpu.VMEM((n_seq, width // tile, batch, tile), f32),
            pltpu.VMEM((n_seq - 1, width // tile, batch, tile), f32),
            pltpu.VMEM((n_seq, batch, size), f32),
            pltpu.VMEM((n_seq - 1, batch, size), f32),
            pltpu.VMEM((n_seq, batch, 128), f32),
            pltpu.VMEM((n_seq, width // tile, batch, tile), bf16),
            pltpu.VMEM((n_seq, batch, size), bf16),
            pltpu.VMEM((heads * batch, size), f32),
            pltpu.VMEM((heads * batch, block), f32),
            pltpu.VMEM((heads * batch, size), f32),
            pltpu.VMEM((n_seq, batch, 128), f32),
            pltpu.VMEM((n_seq - 1, own * batch, size), bf16),
            pltpu.VMEM((n_seq - 1, own * batch, size), bf16),
            pltpu.VMEM((n_seq, width // tile, batch, tile), bf16),
            pltpu.VMEM((batch, columns), f32),
            pltpu.VMEM((n_head, rows, columns), f32),
            pltpu.VMEM((n_head, chunks, rows, columns // chunks), bf16),
            pltpu.VMEM((n_head - 1, chunks, rows, columns // chunks), bf16),
            dma((5 + n_seq + n_seq * width // tile,)),
            dma((n_head,)),
            dma((n_head,)),
            *many, *steps, *steps, *many, *steps, *steps, *many, *many,
            dma((4 * n_head,)),
            dma((4 * n_head,)),
        ],
        compiler_params=pltpu.CompilerParams(
            collective_id=0, has_side_effects=True, vmem_limit_bytes=60 * 1024 * 1024
        ),
    )(hidden, norm_gain.reshape(1, feat), lengths, w_query, w_key, w_value, w_out, key_cache, value_cache)


def program(n_seq, n_head, *args):
    w_query, key_cache = args[2], args[7]
    batch, kv, block, size = key_cache.shape
    heads = w_query.shape[1] // size
    own = max(heads // n_seq, 1)
    fits = (
        own * n_seq == heads
        and (heads // kv) % own == 0
        and 2 * kv == n_seq
        and size == 128
        and block == 128
        and heads <= 64
        and batch % 8 == 0
    )
    return fused(n_seq, n_head, *args) if fits else local(*args)


def solution(mesh):
    return jax.shard_map(
        functools.partial(program, mesh.shape["seq"], mesh.shape["head"]),
        mesh=mesh,
        in_specs=(
            P(("parts", "head"), "seq"),
            P("seq"),
            P("seq", "head"),
            P("seq", "head"),
            P("seq", "head"),
            P("head", "seq"),
            P("parts"),
            P("parts", "head", "seq", None),
            P("parts", "head", "seq", None),
        ),
        out_specs=P(("parts", "head"), "seq"),
        check_vma=False,
    )
```

```python
import functools

import jax
import jax.numpy as jnp
from jax import lax
from jax.experimental import pallas as pl
from jax.experimental.pallas import tpu as pltpu
from jax.sharding import PartitionSpec as P

D = 12288


EPSILON = 1e-05


def joined(value, axis, join):
    pieces = jax.tree.map(lambda part: lax.all_gather(part, axis), value)
    head = jax.tree.map(lambda part: part[0], pieces)
    tail = jax.tree.map(lambda part: part[1:], pieces)
    subtotal, _ = lax.scan(lambda subtotal, slab: (join(subtotal, slab), None), head, tail)
    return subtotal


def join_parts(earlier, later):
    new_max = jnp.maximum(earlier[0], later[0])
    left_factor = jnp.exp(earlier[0] - new_max)
    right_factor = jnp.exp(later[0] - new_max)
    den_total = earlier[1] * left_factor + later[1] * right_factor
    acc_total = earlier[2] * left_factor[..., None] + later[2] * right_factor[..., None]
    return (new_max, den_total, acc_total)


def local(hidden, norm_gain, w_query, w_key, w_value, w_out, lengths, key_cache, value_cache):
    batch_size, kv_local, block_len, head_size = key_cache.shape
    group_size = w_query.shape[1] // (kv_local * head_size)
    token_rows = lax.all_gather(hidden, "head", axis=0, tiled=True)
    widened = token_rows.astype(jnp.float32)
    square_local = jnp.sum(widened * widened, axis=1)
    scaled = (widened * norm_gain).astype(jnp.bfloat16)
    query_part = jnp.dot(scaled, w_query, preferred_element_type=jnp.float32)
    key_part = jnp.dot(scaled, w_key, preferred_element_type=jnp.float32)
    value_part = jnp.dot(scaled, w_value, preferred_element_type=jnp.float32)
    query_factor = float(head_size) ** (-0.5)
    norm_total = lax.psum(square_local, "seq")
    query_sum, key_sum, value_sum = lax.psum((query_part, key_part, value_part), "seq")
    inverse_rms = lax.rsqrt(norm_total / D + EPSILON)[:, None]
    queries = (query_sum * inverse_rms * query_factor).astype(jnp.bfloat16)
    new_keys = (key_sum * inverse_rms).astype(jnp.bfloat16)
    new_values = (value_sum * inverse_rms).astype(jnp.bfloat16)
    grouped = queries.reshape(batch_size, kv_local, group_size, head_size)
    scores = jnp.einsum("bkgd,bkpd->bkgp", grouped, key_cache, preferred_element_type=jnp.float32)
    offset = lax.axis_index("seq") * block_len
    positions = offset + jnp.arange(block_len, dtype=jnp.int32)
    live_mask = (positions[None, :] < lengths[:, None])[:, None, None, :]
    block_max = jnp.max(jnp.where(live_mask, scores, -1e30), axis=-1)
    shifted = jnp.where(live_mask, scores - block_max[..., None], 0.0)
    weights = jnp.where(live_mask, jnp.exp(shifted), 0.0).astype(jnp.bfloat16)
    block_den = jnp.sum(weights.astype(jnp.float32), axis=-1)
    block_acc = jnp.einsum(
        "bkgp,bkpd->bkgd", weights, value_cache, preferred_element_type=jnp.float32
    )
    self_score = jnp.einsum(
        "oips,ois->oip",
        grouped,
        new_keys.reshape(batch_size, kv_local, head_size),
        preferred_element_type=jnp.float32,
    )
    global_max, den_merged, acc_merged = joined(
        (block_max, block_den, block_acc), "seq", join_parts
    )
    top_score = jnp.maximum(global_max, self_score)
    factors = jnp.exp(global_max - top_score)
    den_sum = den_merged * factors
    acc_sum = acc_merged * factors[..., None]
    own_weight = jnp.exp(self_score - top_score)
    denominator = den_sum + own_weight
    numerator = acc_sum + own_weight[..., None] * new_values.reshape(
        batch_size, kv_local, 1, head_size
    ).astype(jnp.float32)
    mixed = (
        (numerator / denominator[..., None])
        .astype(jnp.bfloat16)
        .reshape(batch_size, kv_local * group_size * head_size)
    )
    output = lax.psum_scatter(
        jnp.dot(mixed, w_out, preferred_element_type=jnp.float32),
        "head",
        scatter_dimension=0,
        tiled=True,
    )
    return output.astype(jnp.bfloat16)


MESH = pl.DeviceIdType.MESH


def layer_kernel(
    n_seq, n_head, hid, gain, lens, wq, wk, wv, wo, kc, vc, out,
    hid_buf, x_scr, xs_scr, len_scr, wq_buf, wkv_buf, wo_buf, kc_buf, vc_buf,
    part, rs_buf, kv_part, kv_buf, sq_buf, ag_buf, nk_buf, q_scr, sc_scr, acc_scr, st_buf, acc_send, ra_buf, mix_buf, o_acc, o_own, o_send, o_recv,
    load_sem, hid_send, hid_recv, rs_send, rs_recv, kv_send, kv_recv, sq_send, sq_recv, ag_send, ag_recv, nk_send, nk_recv,
    st_send, st_recv, ra_send, ra_recv, mx_send, mx_recv, os_sem, or_sem,
):
    f32, bf16 = jnp.float32, jnp.bfloat16
    seq, hd = lax.axis_index("seq"), lax.axis_index("head")
    rows, feat = hid.shape
    batch, kv, block, size = kc.shape
    heads = wq.shape[1] // size
    group = heads // kv
    own = heads // n_seq
    width = own * size
    kv_cols = kv * size

    def load(index, source, target):
        copy = pltpu.make_async_copy(source, target, load_sem.at[index])
        copy.start()
        return copy

    def to(axis, index, source, target, send, recv):
        return pltpu.make_async_remote_copy(
            src_ref=source, dst_ref=target, send_sem=send, recv_sem=recv,
            device_id={axis: index}, device_id_type=MESH,
        )

    near = [
        sorted((o for o in range(n_seq) if o != s), key=lambda o: abs(o - s)) for s in range(n_seq)
    ]

    def nearest(j):
        device = jnp.int32(0)
        for s in range(n_seq):
            device = jnp.where(seq == s, near[s][j], device)
        return device

    seq_to = [nearest(n_seq - 2 - j) for j in range(n_seq - 1)] + [seq]
    slots = [lax.rem(seq_to[j] - seq + n_seq - 1, n_seq) for j in range(n_seq - 1)]
    tile = 256 if width % 256 == 0 else size
    pieces = width // tile
    head_to = [lax.rem(hd + j + 1, n_head) for j in range(n_head)]

    own_hidden = load(0, hid, hid_buf.at[hd])
    barrier = pltpu.get_barrier_semaphore()
    for j in range(n_head - 1):
        pl.semaphore_signal(barrier, inc=1, device_id={"head": head_to[j]}, device_id_type=MESH)
    for j in range(n_seq - 1):
        pl.semaphore_signal(barrier, inc=1, device_id={"seq": seq_to[j]}, device_id_type=MESH)
    q_loads = [
        load(
            3 + n * n_seq + j,
            wq.at[:, pl.ds(pl.multiple_of(seq_to[j] * width + n * tile, tile), tile)],
            wq_buf.at[n * n_seq + j],
        )
        for n in range(pieces) for j in range(n_seq)
    ]
    key_load = load(1, wk, wkv_buf.at[:, pl.ds(0, kv_cols)])
    value_load = load(2, wv, wkv_buf.at[:, pl.ds(kv_cols, kv_cols)])
    base = 3 + n_seq * pieces
    kc_load = load(base, kc, kc_buf)
    vc_load = load(base + 1, vc, vc_buf)
    o_loads = [
        load(base + 2 + j, wo.at[pl.ds(j * width, width)], wo_buf.at[j]) for j in range(n_seq)
    ]

    own_hidden.wait()
    pl.semaphore_wait(barrier, n_head + n_seq - 2)

    hid_copies = [
        to("head", head_to[j], hid_buf.at[hd], hid_buf.at[hd], hid_send.at[j], hid_recv.at[j])
        for j in range(n_head - 1)
    ]
    for copy in hid_copies:
        copy.start()
    for b in range(batch):
        len_scr[b : b + 1, :] = jnp.full((1, block), lens[b], jnp.int32)
    for copy in hid_copies:
        copy.wait_recv()
    for j in range(n_head):
        x_scr[j * rows : (j + 1) * rows, :] = hid_buf[j].astype(f32)
    widened = x_scr[...]
    square = jnp.sum(widened * widened, axis=1, keepdims=True)
    sq_buf[n_seq - 1] = jnp.broadcast_to(square, (batch, 128))
    sq_copies = []
    for j in range(n_seq - 1):
        copy = to("seq", seq_to[j], sq_buf.at[n_seq - 1], sq_buf.at[slots[j]], sq_send.at[j], sq_recv.at[slots[j]])
        copy.start()
        sq_copies.append(copy)
    xs_scr[...] = (widened * gain[...]).astype(bf16)

    rs_copies = []
    for n in range(pieces):
        for j in range(n_seq):
            q_loads[n * n_seq + j].wait()
            part[j, n] = jnp.dot(xs_scr[...], wq_buf[n * n_seq + j], preferred_element_type=f32)
            if j < n_seq - 1:
                copy = to(
                    "seq", seq_to[j], part.at[j, n], rs_buf.at[slots[j], n],
                    rs_send.at[j * pieces + n], rs_recv.at[slots[j] * pieces + n],
                )
                copy.start()
                rs_copies.append(copy)
    for copy in sq_copies:
        copy.wait_recv()
    square_sum = sq_buf[0]
    for j in range(1, n_seq):
        square_sum = square_sum + sq_buf[j]
    mean_square = square_sum / (feat * n_seq)
    inverse_rms = lax.rsqrt(mean_square + EPSILON)[:, :1]
    factor = float(size) ** (-0.5)
    ag_copies = []
    for n in range(pieces):
        for j in range(n_seq - 1):
            rs_copies[n * (n_seq - 1) + j].wait_recv()
        total = part[n_seq - 1, n]
        for j in range(n_seq - 1):
            total = total + rs_buf[j, n]
        ag_buf[seq, n] = (total * inverse_rms * factor).astype(bf16)
        for j in range(n_seq - 1):
            copy = to(
                "seq", seq_to[j], ag_buf.at[seq, n], ag_buf.at[seq, n],
                ag_send.at[j * pieces + n], ag_recv.at[slots[j] * pieces + n],
            )
            copy.start()
            ag_copies.append(copy)
    key_load.wait()
    value_load.wait()
    for j in range(n_seq):
        kv_at = pl.ds(pl.multiple_of(seq_to[j] * size, size), size)
        kv_part[j] = jnp.dot(xs_scr[...], wkv_buf[:, kv_at], preferred_element_type=f32)
    kv_copies = []
    for j in range(n_seq - 1):
        copy = to("seq", seq_to[j], kv_part.at[j], kv_buf.at[slots[j]], kv_send.at[j], kv_recv.at[slots[j]])
        copy.start()
        kv_copies.append(copy)
    kc_load.wait()
    vc_load.wait()
    unroll = 6 if batch % 6 == 0 else 1
    sources = n_seq // kv

    def take_queries(source, remote):
        if remote:
            slot = lax.rem(seq - source + n_seq - 1, n_seq)
            for n in range(pieces):
                index = slot * pieces + n
                to(
                    "seq", source, ag_buf.at[source, n], ag_buf.at[source, n], ag_send.at[index], ag_recv.at[index]
                ).wait_recv()
        for i in range(own):
            at = pl.multiple_of((source * own + i) * batch, 8)
            n, first = divmod(i * size, tile)
            q_scr[pl.ds(at, batch), :] = ag_buf[source, n, :, first : first + size].astype(f32)

    def score(k):
        @pl.loop(0, batch // unroll)
        def _(step):
            for u in range(unroll):
                b = step * unroll + u
                at = pl.ds(k * group * batch + b, group, stride=batch)
                sc_scr[at, :] = lax.dot_general(
                    q_scr[at, :].astype(bf16), kc_buf[b, k], (((1,), (1,)), ((), ())),
                    preferred_element_type=f32,
                )

    def accumulate(k):
        @pl.loop(0, batch // unroll)
        def _(step):
            for u in range(unroll):
                b = step * unroll + u
                at = pl.ds(k * group * batch + b, group, stride=batch)
                acc_scr[at, :] = jnp.dot(
                    sc_scr[at, :].astype(bf16), vc_buf[b, k], preferred_element_type=f32
                )

    lane = lax.broadcasted_iota(jnp.int32, (batch, block), 1)
    live = lane + seq * block < len_scr[...]

    def soften(k, stats):
        for g in range(group):
            h = k * group + g
            at = pl.ds(pl.multiple_of(h * batch, 8), batch)
            scores = sc_scr[at, :]
            top = jnp.max(jnp.where(live, scores, -1e30), axis=1, keepdims=True)
            shifted = jnp.where(live, scores - top, 0.0)
            weights = jnp.where(live, jnp.exp(shifted), 0.0).astype(bf16).astype(f32)
            sc_scr[at, :] = weights
            total = jnp.sum(weights, axis=1, keepdims=True)
            stats = jnp.where(lane == h, top, jnp.where(lane == 64 + h, total, stats))
        return stats

    kv_head = (seq * own) // group
    stats = jnp.zeros((batch, 128), f32)
    take_queries(seq, False)
    for t in range(1, sources):
        take_queries(kv_head * sources + lax.rem(seq + t, sources), True)
    score(kv_head)
    stats = soften(kv_head, stats)
    if kv > 1:
        accumulate(kv_head)
    new_part = kv_part[n_seq - 1]
    for copy in kv_copies:
        copy.wait_recv()
    for j in range(n_seq - 1):
        new_part = new_part + kv_buf[j]
    nk_buf[seq] = (new_part * inverse_rms).astype(bf16)
    nk_copies = []
    for j in range(n_seq - 1):
        copy = to("seq", seq_to[j], nk_buf.at[seq], nk_buf.at[seq], nk_send.at[j], nk_recv.at[slots[j]])
        copy.start()
        nk_copies.append(copy)
    others = [lax.rem(kv_head + t, kv) for t in range(1, kv)]
    for k in others:
        for t in range(sources):
            take_queries(k * sources + t, True)
        score(k)
        stats = soften(k, stats)
    st_buf[n_seq - 1] = stats
    st_copies = []
    for j in range(n_seq - 1):
        copy = to("seq", seq_to[j], st_buf.at[n_seq - 1], st_buf.at[slots[j]], st_send.at[j], st_recv.at[slots[j]])
        copy.start()
        st_copies.append(copy)
    for k in others if kv > 1 else [kv_head]:
        accumulate(k)

    ra_copies = []
    part_rows = own * batch
    for j in range(n_seq - 1):
        at = pl.ds(pl.multiple_of(seq_to[j] * part_rows, part_rows), part_rows)
        acc_send[j] = acc_scr[at, :].astype(bf16)
    piece_heads = tile // size
    piece_rows = piece_heads * batch
    for n in range(pieces):
        for j in range(n_seq - 1):
            copy = to(
                "seq", seq_to[j], acc_send.at[j, pl.ds(n * piece_rows, piece_rows)],
                ra_buf.at[slots[j], pl.ds(n * piece_rows, piece_rows)],
                ra_send.at[j * pieces + n], ra_recv.at[slots[j] * pieces + n],
            )
            copy.start()
            ra_copies.append(copy)

    for copy in nk_copies:
        copy.wait_recv()
    new_key = nk_buf[kv_head].astype(f32)
    new_value = nk_buf[kv + kv_head].astype(f32)
    own_at = pl.multiple_of(seq * part_rows, part_rows)
    self_score = jnp.zeros((batch, 128), f32)
    for i in range(own):
        query = q_scr[pl.ds(own_at + i * batch, batch), :]
        score = jnp.sum(query * new_key, axis=1, keepdims=True)
        self_score = jnp.where(lane == i, score, self_score)
    for copy in st_copies:
        copy.wait_recv()
    shift = lax.rem(128 - seq * own, 128)
    maxes = [pltpu.roll(st_buf[j], shift, 1) for j in range(n_seq)]
    dens = [pltpu.roll(m, 64, 1) for m in maxes]
    top_score = self_score
    for m in maxes:
        top_score = jnp.maximum(top_score, m)
    factors = [jnp.exp(m - top_score) for m in maxes]
    own_weight = jnp.exp(self_score - top_score)
    denominator = own_weight
    for f, d in zip(factors, dens):
        denominator = denominator + f * d
    own_weight = own_weight / denominator
    factors = [f / denominator for f in factors]
    mx_copies = []
    for n in range(pieces):
        for j in range(n_seq - 1):
            ra_copies[n * (n_seq - 1) + j].wait_recv()
        for p in range(piece_heads):
            i = n * piece_heads + p
            mixed = own_weight[:, i : i + 1] * new_value
            mixed += factors[n_seq - 1][:, i : i + 1] * acc_scr[pl.ds(own_at + i * batch, batch), :]
            for j in range(n_seq - 1):
                mixed += factors[j][:, i : i + 1] * ra_buf[j, i * batch : (i + 1) * batch, :].astype(f32)
            mix_buf[seq, n, :, p * size : (p + 1) * size] = mixed.astype(bf16)
        for j in range(n_seq - 1):
            copy = to(
                "seq", seq_to[j], mix_buf.at[seq, n], mix_buf.at[seq, n],
                mx_send.at[j * pieces + n], mx_recv.at[slots[j] * pieces + n],
            )
            copy.start()
            mx_copies.append(copy)
    for copy in o_loads:
        copy.wait()

    columns = wo.shape[1]
    chunks = 4 if columns % 512 == 0 else 1
    chunk = columns // chunks

    def mix_of(source):
        return jnp.concatenate([mix_buf[source, n] for n in range(pieces)], axis=1)

    def o_copy(c, r):
        index = c * n_head + r
        return to(
            "head", head_to[r], o_send.at[head_to[r], c], o_recv.at[r, c], os_sem.at[index], or_sem.at[index]
        )

    for j in range(n_seq):
        source = seq
        if j > 0:
            source = nearest(j - 1)
            slot = lax.rem(seq - source + n_seq - 1, n_seq)
            for n in range(pieces):
                index = slot * pieces + n
                to(
                    "seq", source, mix_buf.at[source, n], mix_buf.at[source, n], mx_send.at[index], mx_recv.at[index]
                ).wait_recv()
        last = j == n_seq - 1

        @pl.loop(0, chunks)
        def _(c):
            cols = pl.ds(pl.multiple_of(c * chunk, 128), chunk)
            value = jnp.dot(mix_of(source), wo_buf[source, :, cols], preferred_element_type=f32)
            if j > 0:
                value = o_acc[:, cols] + value
            if not last:
                o_acc[:, cols] = value
                return
            for r in range(n_head):
                o_own[r, :, cols] = value[r * rows : (r + 1) * rows]
                o_send[r, c] = value[r * rows : (r + 1) * rows].astype(bf16)
            for r in range(n_head - 1):
                o_copy(c, r).start()

    for c in range(chunks):
        cols = slice(c * chunk, (c + 1) * chunk)
        for r in range(n_head - 1):
            o_copy(c, r).wait_recv()
        total = o_own[hd, :, cols]
        for r in range(n_head - 1):
            total = total + o_recv[r, c].astype(f32)
        out[:, cols] = total.astype(bf16)
    for copy in hid_copies + rs_copies + kv_copies + sq_copies + ag_copies + nk_copies + st_copies + ra_copies + mx_copies:
        copy.wait_send()
    for c in range(chunks):
        for r in range(n_head - 1):
            o_copy(c, r).wait_send()


def fused(n_seq, n_head, hidden, norm_gain, w_query, w_key, w_value, w_out, lengths, key_cache, value_cache):
    rows, feat = hidden.shape
    batch, kv, block, size = key_cache.shape
    heads = w_query.shape[1] // size
    own = heads // n_seq
    width = own * size
    tile = 256 if width % 256 == 0 else size
    columns = w_out.shape[1]
    chunks = 4 if columns % 512 == 0 else 1
    f32, bf16 = jnp.float32, jnp.bfloat16
    hbm = pl.BlockSpec(memory_space=pl.ANY)
    vmem = pl.BlockSpec(memory_space=pltpu.VMEM)
    smem = pl.BlockSpec(memory_space=pltpu.SMEM)
    dma = pltpu.SemaphoreType.DMA
    steps = [dma((n_seq,)), dma((n_seq,))]
    many = [dma((n_seq * width // tile,)), dma((n_seq * width // tile,))]
    return pl.pallas_call(
        functools.partial(layer_kernel, n_seq, n_head),
        out_shape=jax.ShapeDtypeStruct((rows, columns), bf16),
        in_specs=[hbm, vmem, smem] + [hbm] * 6,
        out_specs=vmem,
        scratch_shapes=[
            pltpu.VMEM((n_head, rows, feat), bf16),
            pltpu.VMEM((batch, feat), f32),
            pltpu.VMEM((batch, feat), bf16),
            pltpu.VMEM((batch, block), jnp.int32),
            pltpu.VMEM((n_seq * width // tile, feat, tile), bf16),
            pltpu.VMEM((feat, 2 * kv * size), bf16),
            pltpu.VMEM((n_seq, width, columns), bf16),
            pltpu.VMEM(key_cache.shape, bf16),
            pltpu.VMEM(value_cache.shape, bf16),
            pltpu.VMEM((n_seq, width // tile, batch, tile), f32),
            pltpu.VMEM((n_seq - 1, width // tile, batch, tile), f32),
            pltpu.VMEM((n_seq, batch, size), f32),
            pltpu.VMEM((n_seq - 1, batch, size), f32),
            pltpu.VMEM((n_seq, batch, 128), f32),
            pltpu.VMEM((n_seq, width // tile, batch, tile), bf16),
            pltpu.VMEM((n_seq, batch, size), bf16),
            pltpu.VMEM((heads * batch, size), f32),
            pltpu.VMEM((heads * batch, block), f32),
            pltpu.VMEM((heads * batch, size), f32),
            pltpu.VMEM((n_seq, batch, 128), f32),
            pltpu.VMEM((n_seq - 1, own * batch, size), bf16),
            pltpu.VMEM((n_seq - 1, own * batch, size), bf16),
            pltpu.VMEM((n_seq, width // tile, batch, tile), bf16),
            pltpu.VMEM((batch, columns), f32),
            pltpu.VMEM((n_head, rows, columns), f32),
            pltpu.VMEM((n_head, chunks, rows, columns // chunks), bf16),
            pltpu.VMEM((n_head - 1, chunks, rows, columns // chunks), bf16),
            dma((5 + n_seq + n_seq * width // tile,)),
            dma((n_head,)),
            dma((n_head,)),
            *many, *steps, *steps, *many, *steps, *steps, *many, *many,
            dma((4 * n_head,)),
            dma((4 * n_head,)),
        ],
        compiler_params=pltpu.CompilerParams(
            collective_id=0, has_side_effects=True, vmem_limit_bytes=60 * 1024 * 1024
        ),
    )(hidden, norm_gain.reshape(1, feat), lengths, w_query, w_key, w_value, w_out, key_cache, value_cache)


def program(n_seq, n_head, *args):
    w_query, key_cache = args[2], args[7]
    batch, kv, block, size = key_cache.shape
    heads = w_query.shape[1] // size
    own = max(heads // n_seq, 1)
    fits = (
        own * n_seq == heads
        and (heads // kv) % own == 0
        and 2 * kv == n_seq
        and size == 128
        and block == 128
        and heads <= 64
        and batch % 8 == 0
    )
    return fused(n_seq, n_head, *args) if fits else local(*args)


def solution(mesh):
    return jax.shard_map(
        functools.partial(program, mesh.shape["seq"], mesh.shape["head"]),
        mesh=mesh,
        in_specs=(
            P(("parts", "head"), "seq"),
            P("seq"),
            P("seq", "head"),
            P("seq", "head"),
            P("seq", "head"),
            P("head", "seq"),
            P("parts"),
            P("parts", "head", "seq", None),
            P("parts", "head", "seq", None),
        ),
        out_specs=P(("parts", "head"), "seq"),
        check_vma=False,
    )
```
